256 devices in a mesh: expert: 64 (over x, z, core), replica: 4 (over y).
Axes of the slice: x: 4, y: 4, z: 8, core: 2. Of those that a mesh axis runs over, the one named last changes fastest.
Arguments:
- tokens: bfloat16 [8192, 2560], P('expert'), may hold values from -6 to 6
- expert_ids: int32 [8192, 6], P('expert'), may hold values from 0 to 63, all different within a row; in each aligned block of 128 rows (0 to 127, 128 to 255, ...) at most 16 rows name the same one
- route_weights: float32 [8192, 6], P('expert'), may hold values from 0.05 to 0.5
- w_gate: bfloat16 [64, 2560, 1536], P('expert', None, 'replica'), may hold values from -0.125 to 0.125
- w_up: bfloat16 [64, 2560, 1536], P('expert', None, 'replica'), may hold values from -0.125 to 0.125
- w_down: bfloat16 [64, 1536, 2560], P('expert', 'replica'), may hold values from -0.15625 to 0.15625
- cotangent: bfloat16 [8192, 2560], P('expert'), may hold values from -6 to 6
Outputs:
- mixed: bfloat16 [8192, 2560], P('expert', 'replica')
- tokens_grad: bfloat16 [8192, 2560], P('expert', 'replica')
The draws below stay inside these ranges and needn't reach their ends.
Inputs may be any that keep to these rules, and one draw needn't show every extreme that they name: `expert_ids`: each row names 6 different experts. In each aligned block of 128 rows no expert is named by more than 16 rows, a bound that some block reaches.
All inputs are finite; a program needn't handle non-finite values.
Results may differ from the reference program's by a relative error of at most 0.0064.
Values may be sent and summed in bfloat16 or wider, within the bound.
No kernel may reach another device: no remote copies, remote signals or barrier semaphores. Data moves between devices by JAX's collectives and lax.ppermute only.
A program may use at most 128 MiB of HBM per device.

```python
import math
import jax
import jax.numpy as jnp
import numpy as np
from jax import lax

D = 2560
FF = 1536
TOP = 6
TOK_DEV = 128
EXPERTS = 64
CAP = 16
TOKENS = 8192


def shard_levels(stream_key, extent, split, smallest, top_value):
    gain, own = 1.0, jax.random.fold_in(stream_key, 6)
    for axis_at, shards_of in split:
        draws = jnp.exp(jax.random.uniform(jax.random.fold_in(own, axis_at), (shards_of,), jnp.float32, smallest / len(split), top_value / len(split)))
        gain = gain * jnp.repeat(draws, extent[axis_at] // shards_of).reshape([-1 if axis == axis_at else 1 for axis in range(len(extent))])
    return gain


def shared_out(rng, own, number, rows, amount, top, reach, lean):
    order = jax.random.permutation(rng, amount)
    heavy_load, common = shares(amount, rows * top, reach, lean, True), shares(amount, rows * top, reach, lean, False)
    places = jnp.arange(amount)

    def named(tallies, offset_by):
        used = int((tallies > 0).sum())
        fixed = max(1, used // 4)
        shifted = fixed + (places - fixed + offset_by * (used - fixed)) % max(1, amount - fixed)
        return jnp.zeros((amount,), jnp.int32).at[order[jnp.where(places < fixed, places, shifted)]].set(jnp.asarray(tallies, jnp.int32))

    tallies = jnp.where(number % 4 == 0, named(heavy_load, number // 4), named(common, number - number // 4 - 1))
    mixed = jax.random.permutation(jax.random.fold_in(own, 3), amount)
    giver, taker = mixed[0:amount // 2 * 2:2], mixed[1:amount // 2 * 2:2]
    margin = jnp.minimum(tallies[giver] - 1, reach - tallies[taker]) // 2
    margin = jnp.where((giver == order[0]) | (taker == order[0]) | (tallies[taker] == 0), 0, jnp.maximum(margin, 0))
    shifted = jax.random.randint(jax.random.fold_in(own, 4), (amount // 2,), 0, 1 << 20) % (margin + 1)
    tallies = tallies.at[giver].add(-shifted).at[taker].add(shifted)
    labels = jnp.searchsorted(jnp.cumsum(tallies), jnp.arange(rows * top), side="right").astype(jnp.int32)
    listing = labels.reshape(top, rows).T
    listing = listing[jax.random.permutation(jax.random.fold_in(own, 1), rows)]
    offset_by = jax.random.randint(jax.random.fold_in(own, 2), (rows, 1), 0, top)
    return jnp.take_along_axis(listing, (jnp.arange(top)[None, :] + offset_by) % top, axis=1)


def shares(number_of, total, reach, skew, full):
    weights = [(1 << 20) // math.isqrt(grade ** skew) + 1 for grade in range(1, number_of + 1)]
    largest = reach if full else min(reach, max(-(-total // number_of), total * weights[0] // sum(weights)))
    least = 1 if total - largest >= number_of - 1 else 0
    holding, rest = [largest] + [least] * (number_of - 1), total - largest - least * (number_of - 1)
    while rest > 0:
        movable = [i for i in range(1, number_of) if holding[i] < largest] or [i for i in range(1, number_of) if holding[i] < reach]
        whole, budget = sum([weights[i] for i in movable]), rest
        for i in movable:
            addition = min(reach - holding[i], max(1, budget * weights[i] // whole), rest)
            holding[i] = holding[i] + addition
            rest = rest - addition
    return np.array(holding)


def bell_draw(key, dims, width, bound, shards=(), kind=jnp.bfloat16):
    array = width * jax.random.normal(key, dims, jnp.float32)
    if shards:
        array = array * shard_levels(key, dims, shards, -0.22, 0.18)
    return jnp.clip(array, -bound, bound).astype(kind)


def setup_inputs(seed: int = 0) -> dict:
    arg_keys = jax.random.split(jax.random.key(seed), 8)
    tokens = bell_draw(arg_keys[0], (TOKENS, D), 1.0, 6.0, ((0, 64),))
    expert_ids_keys = jax.random.split(jax.random.fold_in(arg_keys[1], 1), TOKENS // TOK_DEV)
    expert_ids_turns = jax.random.permutation(jax.random.fold_in(arg_keys[1], 3), TOKENS // TOK_DEV)
    expert_ids = jax.vmap(lambda own, number: shared_out(jax.random.fold_in(arg_keys[1], 2), own, number, TOK_DEV, EXPERTS, TOP, CAP, 2))(expert_ids_keys, expert_ids_turns).reshape((TOKENS, TOP))
    route_weights = jnp.clip(0.05 + 0.45 * jax.random.uniform(arg_keys[2], (TOKENS, TOP), jnp.float32) ** shard_levels(arg_keys[2], (TOKENS, TOP), ((0, 64),), -0.2, 0.2), 0.05, 0.5)
    w_gate = bell_draw(arg_keys[3], (EXPERTS, D, FF), D ** -0.5, 0.125, ((0, 64), (2, 4)))
    w_up = bell_draw(arg_keys[4], (EXPERTS, D, FF), D ** -0.5, 0.125, ((0, 64), (2, 4)))
    w_down = bell_draw(arg_keys[5], (EXPERTS, FF, D), FF ** -0.5, 0.15625, ((0, 64), (1, 4)))
    cotangent = bell_draw(arg_keys[6], (TOKENS, D), 1.0, 6.0, ((0, 64),))
    return {"tokens": tokens, "expert_ids": expert_ids, "route_weights": route_weights, "w_gate": w_gate, "w_up": w_up, "w_down": w_down, "cotangent": cotangent}


def reference(tokens, expert_ids, route_weights, w_gate, w_up, w_down, cotangent):
    flat_ids = expert_ids.reshape(-1)
    flat_weights = route_weights.reshape(-1)
    limit = EXPERTS * CAP

    def per_expert(carry, expert):
        mixed_acc, grad_acc = carry
        chosen = flat_ids == expert
        taken = jnp.nonzero(chosen, size=limit, fill_value=0)[0].astype(jnp.int32)
        count = jnp.sum(chosen.astype(jnp.int32))
        valid = (jnp.arange(limit, dtype=jnp.int32) < count).astype(jnp.float32)
        token_rows = (taken // TOP).astype(jnp.int32)
        weight = flat_weights[taken]
        rows = tokens[token_rows]
        gate_w = w_gate[expert]
        up_w = w_up[expert]
        down_w = w_down[expert]
        gate = jnp.dot(rows, gate_w, preferred_element_type=jnp.float32)
        up = jnp.dot(rows, up_w, preferred_element_type=jnp.float32)
        sig = jax.nn.sigmoid(gate)
        act = gate * sig
        hidden = (act * up).astype(jnp.bfloat16)
        expert_out = jnp.dot(hidden, down_w, preferred_element_type=jnp.float32).astype(jnp.bfloat16)
        contrib = expert_out.astype(jnp.float32) * (weight * valid)[:, None]
        mixed_acc = mixed_acc.at[token_rows].add(contrib)
        slot_grad = (cotangent[token_rows].astype(jnp.float32) * weight[:, None]).astype(jnp.bfloat16)
        hidden_grad = jnp.dot(slot_grad, down_w.T, preferred_element_type=jnp.float32)
        gate_grad = (hidden_grad * up * sig * (1.0 + gate * (1.0 - sig))).astype(jnp.bfloat16)
        up_grad = (hidden_grad * act).astype(jnp.bfloat16)
        slot_input = jnp.dot(gate_grad, gate_w.T, preferred_element_type=jnp.float32)
        slot_input = slot_input + jnp.dot(up_grad, up_w.T, preferred_element_type=jnp.float32)
        slot_input = slot_input.astype(jnp.bfloat16).astype(jnp.float32) * valid[:, None]
        grad_acc = grad_acc.at[token_rows].add(slot_input)
        return (mixed_acc, grad_acc), None

    start = (jnp.zeros(tokens.shape, jnp.float32), jnp.zeros(tokens.shape, jnp.float32))
    (mixed_acc, grad_acc), _ = lax.scan(per_expert, start, jnp.arange(EXPERTS, dtype=jnp.int32))
    return mixed_acc.astype(jnp.bfloat16), grad_acc.astype(jnp.bfloat16)
```

```python
import jax
import jax.numpy as jnp
from jax import lax
from jax.sharding import PartitionSpec as P


BF = jnp.bfloat16
F32 = jnp.float32
B_PAIRS = [(0, 1), (1, 0), (2, 3), (3, 2)]
A_PAIRS = [(0, 3), (3, 0), (1, 2), (2, 1)]


def swap_b(value):
    return lax.ppermute(value, "replica", B_PAIRS)


def swap_a(value):
    return lax.ppermute(value, "replica", A_PAIRS)


def dot(lhs, rhs, ldim=1, rdim=0):
    return lax.dot_general(lhs, rhs, (((ldim,), (rdim,)), ((), ())), preferred_element_type=F32)


def halves(value, axis, first):
    low, high = jnp.split(value, 2, axis=axis)
    return jnp.where(first == 0, low, high), jnp.where(first == 0, high, low)


def exchange(rows, num_experts):
    width = rows.shape[1]
    moved = lax.all_to_all(
        rows.reshape(num_experts, -1, width), "expert", split_axis=0, concat_axis=0, tiled=True
    )
    return moved.reshape(-1, width)


def layer(tokens, expert_ids, route_weights, w_gate, w_up, w_down, cotangent):
    num_experts = lax.axis_size("expert")
    tok_rows, top = expert_ids.shape
    capacity = tok_rows * top * 4 // (num_experts * 3)
    slots = capacity // 2
    y = lax.axis_index("replica")
    a = y >> 1
    b = ((y + 1) >> 1) & 1
    gate_w, up_w, down_w = w_gate[0], w_up[0], w_down[0]

    gate_b = swap_b(gate_w)
    up_b = swap_b(up_w)
    down_own, down_far = halves(down_w, 1, a)
    down_a = swap_a(down_far)
    down_b = swap_b(down_own)
    down_ab = swap_b(down_a)

    experts = jnp.arange(num_experts, dtype=jnp.int32)
    hit = expert_ids.T[None, :, :] == experts[:, None, None]
    chosen = jnp.sum(hit.astype(F32), axis=1)
    weight = jnp.sum(jnp.where(hit, route_weights.T[None, :, :], 0.0), axis=1)
    before = jnp.arange(tok_rows)[:, None] < jnp.arange(tok_rows)[None, :]
    rank = dot(chosen.astype(BF), before.astype(BF))
    place = jnp.where(chosen > 0, rank.astype(jnp.int32) - slots * b, -1)
    pick = place[:, None, :] == jnp.arange(slots, dtype=jnp.int32)[None, :, None]
    pick_w = jnp.where(pick, weight[:, None, :], 0.0).reshape(-1, tok_rows)
    pick = pick.astype(BF).reshape(-1, tok_rows)
    slot_weight = jnp.sum(pick_w, axis=1, keepdims=True)
    pick_hi = pick_w.astype(BF)
    pick_lo = (pick_w - pick_hi.astype(F32)).astype(BF)

    tok_half, _ = halves(tokens, 1, a)
    cot_half, _ = halves(cotangent, 1, a)
    packed = dot(pick, tok_half).astype(BF)
    rows_near = exchange(packed, num_experts)
    rows_far = swap_a(rows_near)
    packed_grad = (dot(pick, cot_half) * slot_weight).astype(BF)
    grad_rows = exchange(packed_grad, num_experts)

    gate_1n, gate_1f = halves(gate_w, 0, a)
    up_1n, up_1f = halves(up_w, 0, a)
    gate_2n, gate_2f = halves(gate_b, 0, a)
    up_2n, up_2f = halves(up_b, 0, a)

    def forward(gate_n, gate_f, up_n, up_f):
        gate = dot(rows_near, gate_n) + dot(rows_far, gate_f)
        up = dot(rows_near, up_n) + dot(rows_far, up_f)
        hidden = (gate * jax.nn.sigmoid(gate) * up).astype(BF)
        return lax.optimization_barrier((gate, up, hidden))

    def backward(hidden_grad, gate, up):
        sig = jax.nn.sigmoid(gate)
        act = gate * sig
        gate_grad = (hidden_grad * up * sig * (1.0 + gate * (1.0 - sig))).astype(BF)
        return gate_grad, (hidden_grad * act).astype(BF)

    gate_1, up_1, hidden_1 = forward(gate_1n, gate_1f, up_1n, up_1f)
    gate_2, up_2, hidden_2 = forward(gate_2n, gate_2f, up_2n, up_2f)
    hidden_3 = swap_a(hidden_1)
    hidden_4 = swap_a(hidden_2)
    hgrad_3 = dot(grad_rows, down_a, 1, 1).astype(BF)
    hgrad_3 = swap_a(hgrad_3)
    hgrad_4 = dot(grad_rows, down_ab, 1, 1).astype(BF)
    hgrad_4 = swap_a(hgrad_4)

    mixed_rows = dot(hidden_1, down_own) + dot(hidden_3, down_a)
    mixed_rows = mixed_rows + dot(hidden_2, down_b) + dot(hidden_4, down_ab)
    mixed_back = exchange(mixed_rows.astype(BF), num_experts)

    hgrad_1 = dot(grad_rows, down_own, 1, 1)
    hgrad_2 = dot(grad_rows, down_b, 1, 1)
    gg_1, ug_1 = backward(hgrad_1 + hgrad_3.astype(F32), gate_1, up_1)
    gg_2, ug_2 = backward(hgrad_2 + hgrad_4.astype(F32), gate_2, up_2)
    far = dot(gg_1, gate_1f, 1, 1) + dot(ug_1, up_1f, 1, 1)
    far = far + dot(gg_2, gate_2f, 1, 1) + dot(ug_2, up_2f, 1, 1)
    far = far.astype(BF)
    far = swap_a(far)
    near = dot(gg_1, gate_1n, 1, 1) + dot(ug_1, up_1n, 1, 1)
    near = near + dot(gg_2, gate_2n, 1, 1) + dot(ug_2, up_2n, 1, 1)
    near = near + far.astype(F32)
    grad_back = exchange(near.astype(BF), num_experts)

    def finish(partial):
        keep, give = halves(partial, 1, y & 1)
        return (keep + swap_b(give.astype(BF)).astype(F32)).astype(BF)

    mixed = finish(dot(pick_hi, mixed_back, 0, 0) + dot(pick_lo, mixed_back, 0, 0))
    tokens_grad = finish(dot(pick, grad_back, 0, 0))
    return (mixed, tokens_grad)


def solution(mesh):
    in_specs = (
        P("expert", None),
        P("expert", None),
        P("expert", None),
        P("expert", None, "replica"),
        P("expert", None, "replica"),
        P("expert", "replica", None),
        P("expert", None),
    )
    out_specs = (P("expert", "replica"), P("expert", "replica"))
    return jax.shard_map(
        layer, mesh=mesh, in_specs=in_specs, out_specs=out_specs, check_vma=False
    )
```

```python
import jax
import jax.numpy as jnp
from jax import lax
from jax.sharding import PartitionSpec as P


BF = jnp.bfloat16
F32 = jnp.float32
B_PAIRS = [(0, 1), (1, 0), (2, 3), (3, 2)]
A_PAIRS = [(0, 3), (3, 0), (1, 2), (2, 1)]


def swap_b(value):
    return lax.ppermute(value, "replica", B_PAIRS)


def swap_a(value):
    return lax.ppermute(value, "replica", A_PAIRS)


def dot(lhs, rhs, ldim=1, rdim=0):
    return lax.dot_general(lhs, rhs, (((ldim,), (rdim,)), ((), ())), preferred_element_type=F32)


def halves(value, axis, first):
    low, high = jnp.split(value, 2, axis=axis)
    return jnp.where(first == 0, low, high), jnp.where(first == 0, high, low)


def exchange(rows, num_experts):
    width = rows.shape[1]
    moved = lax.all_to_all(
        rows.reshape(num_experts, -1, width), "expert", split_axis=0, concat_axis=0, tiled=True
    )
    return moved.reshape(-1, width)


def layer(tokens, expert_ids, route_weights, w_gate, w_up, w_down, cotangent):
    num_experts = lax.axis_size("expert")
    tok_rows, top = expert_ids.shape
    capacity = tok_rows * top * 4 // (num_experts * 3)
    slots = capacity // 2
    y = lax.axis_index("replica")
    a = y >> 1
    b = ((y + 1) >> 1) & 1
    gate_w, up_w, down_w = w_gate[0], w_up[0], w_down[0]

    gate_b = swap_b(gate_w)
    up_b = swap_b(up_w)
    down_own, down_far = halves(down_w, 1, a)
    down_a = swap_a(down_far)
    down_ab = swap_b(down_a)
    cut = down_own.shape[0] * 2 // 3
    down_b1 = swap_b(down_own[:cut])
    down_b2 = swap_b(down_own[cut:])

    experts = jnp.arange(num_experts, dtype=jnp.int32)
    hit = expert_ids.T[None, :, :] == experts[:, None, None]
    chosen = jnp.sum(hit.astype(F32), axis=1)
    weight = jnp.sum(jnp.where(hit, route_weights.T[None, :, :], 0.0), axis=1)
    before = jnp.arange(tok_rows)[:, None] < jnp.arange(tok_rows)[None, :]
    rank = dot(chosen.astype(BF), before.astype(BF))
    place = jnp.where(chosen > 0, rank.astype(jnp.int32) - slots * b, -1)
    pick = place[:, None, :] == jnp.arange(slots, dtype=jnp.int32)[None, :, None]
    pick_w = jnp.where(pick, weight[:, None, :], 0.0).reshape(-1, tok_rows)
    pick = pick.astype(BF).reshape(-1, tok_rows)
    slot_weight = jnp.sum(pick_w, axis=1, keepdims=True)
    pick_hi = pick_w.astype(BF)
    pick_lo = (pick_w - pick_hi.astype(F32)).astype(BF)

    tok_half, _ = halves(tokens, 1, a)
    cot_half, _ = halves(cotangent, 1, a)
    packed = dot(pick, tok_half).astype(BF)
    rows_near = exchange(packed, num_experts)
    rows_far = swap_a(rows_near)
    packed_grad = (dot(pick, cot_half) * slot_weight).astype(BF)
    grad_rows = exchange(packed_grad, num_experts)

    gate_1n, gate_1f = halves(gate_w, 0, a)
    up_1n, up_1f = halves(up_w, 0, a)
    gate_2n, gate_2f = halves(gate_b, 0, a)
    up_2n, up_2f = halves(up_b, 0, a)

    def forward(gate_n, gate_f, up_n, up_f):
        gate = dot(rows_near, gate_n) + dot(rows_far, gate_f)
        up = dot(rows_near, up_n) + dot(rows_far, up_f)
        hidden = (gate * jax.nn.sigmoid(gate) * up).astype(BF)
        return lax.optimization_barrier((gate, up, hidden))

    def backward(hidden_grad, gate, up):
        sig = jax.nn.sigmoid(gate)
        act = gate * sig
        gate_grad = (hidden_grad * up * sig * (1.0 + gate * (1.0 - sig))).astype(BF)
        return gate_grad, (hidden_grad * act).astype(BF)

    late_n = lax.optimization_barrier(jnp.concatenate([gate_2n[:, cut:], up_2n[:, cut:]], axis=1))
    late_f = lax.optimization_barrier(jnp.concatenate([gate_2f[:, cut:], up_2f[:, cut:]], axis=1))

    gate_1, up_1, hidden_1 = forward(gate_1n, gate_1f, up_1n, up_1f)
    gate_2, up_2, hidden_2 = forward(gate_2n, gate_2f, up_2n, up_2f)
    hidden_3 = swap_a(hidden_1)
    hidden_4 = swap_a(hidden_2)
    hgrad_3 = dot(grad_rows, down_a, 1, 1).astype(BF)
    hgrad_3 = swap_a(hgrad_3)
    hgrad_4 = dot(grad_rows, down_ab, 1, 1).astype(BF)
    hgrad_4 = swap_a(hgrad_4)

    mixed_rows = dot(hidden_1, down_own) + dot(hidden_3, down_a)
    mixed_rows = mixed_rows + dot(hidden_2[:, :cut], down_b1) + dot(hidden_4, down_ab)
    mixed_rows = lax.optimization_barrier(mixed_rows)
    mixed_rows = mixed_rows + dot(hidden_2[:, cut:], down_b2)
    mixed_back = exchange(mixed_rows.astype(BF), num_experts)

    hgrad_1 = dot(grad_rows, down_own, 1, 1)
    gg_1, ug_1 = backward(hgrad_1 + hgrad_3.astype(F32), gate_1, up_1)
    hgrad_2 = dot(grad_rows, down_b1, 1, 1)
    gg_2, ug_2 = backward(hgrad_2 + hgrad_4[:, :cut].astype(F32), gate_2[:, :cut], up_2[:, :cut])
    hgrad_2 = dot(grad_rows, down_b2, 1, 1)
    late = backward(hgrad_2 + hgrad_4[:, cut:].astype(F32), gate_2[:, cut:], up_2[:, cut:])
    grads_3 = jnp.concatenate(late, axis=1)
    far = dot(gg_1, gate_1f, 1, 1) + dot(ug_1, up_1f, 1, 1)
    far = far + dot(gg_2, gate_2f[:, :cut], 1, 1) + dot(ug_2, up_2f[:, :cut], 1, 1)
    far = lax.optimization_barrier(far)
    far = (far + dot(grads_3, late_f, 1, 1)).astype(BF)
    far = swap_a(far)
    near = dot(gg_1, gate_1n, 1, 1) + dot(ug_1, up_1n, 1, 1)
    near = near + dot(gg_2, gate_2n[:, :cut], 1, 1) + dot(ug_2, up_2n[:, :cut], 1, 1)
    near = lax.optimization_barrier(near)
    near = near + dot(grads_3, late_n, 1, 1)
    near = near + far.astype(F32)
    grad_back = exchange(near.astype(BF), num_experts)

    def finish(partial):
        keep, give = halves(partial, 1, y & 1)
        return (keep + swap_b(give.astype(BF)).astype(F32)).astype(BF)

    mixed = finish(dot(pick_hi, mixed_back, 0, 0) + dot(pick_lo, mixed_back, 0, 0))
    tokens_grad = finish(dot(pick, grad_back, 0, 0))
    return (mixed, tokens_grad)


def solution(mesh):
    in_specs = (
        P("expert", None),
        P("expert", None),
        P("expert", None),
        P("expert", None, "replica"),
        P("expert", None, "replica"),
        P("expert", "replica", None),
        P("expert", None),
    )
    out_specs = (P("expert", "replica"), P("expert", "replica"))
    return jax.shard_map(layer, mesh=mesh, in_specs=in_specs, out_specs=out_specs, check_vma=False)
```

```python
import jax
import jax.numpy as jnp
from jax import lax
from jax.experimental import pallas as pl
from jax.experimental.pallas import tpu as pltpu
from jax.sharding import PartitionSpec as P


BF = jnp.bfloat16
F32 = jnp.float32
B_PAIRS = [(0, 1), (1, 0), (2, 3), (3, 2)]
A_PAIRS = [(0, 3), (3, 0), (1, 2), (2, 1)]


def swap_b(value):
    return lax.ppermute(value, "replica", B_PAIRS)


def swap_a(value):
    return lax.ppermute(value, "replica", A_PAIRS)


def dot(lhs, rhs, ldim=1, rdim=0):
    return lax.dot_general(lhs, rhs, (((ldim,), (rdim,)), ((), ())), preferred_element_type=F32)


def halves(value, axis, first):
    low, high = jnp.split(value, 2, axis=axis)
    return jnp.where(first == 0, low, high), jnp.where(first == 0, high, low)


def exchange(rows, num_experts):
    width = rows.shape[1]
    moved = lax.all_to_all(
        rows.reshape(num_experts, -1, width), "expert", split_axis=0, concat_axis=0, tiled=True
    )
    return moved.reshape(-1, width)


def near_first(j, a):
    return jnp.where(j < 2, 2 * a + j, 2 * (1 - a) + j - 2)


def act_hidden(gate, up):
    return (gate * jax.nn.sigmoid(gate) * up).astype(BF)


def forward_near(a, near, gate_w, up_w):
    rows, half = near.shape
    hidden_units = gate_w.shape[1]
    step = half // 2

    def kernel(a_ref, near_ref, gate_w_ref, up_w_ref, gate_ref, up_ref):
        gate = dot(near_ref[...], gate_w_ref[...])
        up = dot(near_ref[...], up_w_ref[...])

        @pl.when(pl.program_id(0) == 0)
        def _():
            gate_ref[...] = gate
            up_ref[...] = up

        @pl.when(pl.program_id(0) == 1)
        def _():
            gate_ref[...] += gate
            up_ref[...] += up

    whole = pl.BlockSpec((rows, hidden_units), lambda j, a_ref: (0, 0))
    weight = pl.BlockSpec((step, hidden_units), lambda j, a_ref: (near_first(j, a_ref[0]), 0))
    return pl.pallas_call(
        kernel,
        grid_spec=pltpu.PrefetchScalarGridSpec(
            num_scalar_prefetch=1,
            grid=(2,),
            in_specs=[pl.BlockSpec((rows, step), lambda j, a_ref: (0, j)), weight, weight],
            out_specs=[whole, whole],
        ),
        out_shape=[jax.ShapeDtypeStruct((rows, hidden_units), F32)] * 2,
        name="forward_near",
    )(a, near, gate_w, up_w)


def forward_far(a, far, gate_near, up_near, gate_w, up_w):
    rows, half = far.shape
    hidden_units = gate_w.shape[1]
    step = half // 2

    def kernel(a_ref, far_ref, gn_ref, un_ref, gate_w_ref, up_w_ref, gate_ref, up_ref, hidden_ref):
        @pl.when(pl.program_id(0) == 0)
        def _():
            gate_ref[...] = gn_ref[...] + dot(far_ref[...], gate_w_ref[...])
            up_ref[...] = un_ref[...] + dot(far_ref[...], up_w_ref[...])

        @pl.when(pl.program_id(0) == 1)
        def _():
            gate = gate_ref[...] + dot(far_ref[...], gate_w_ref[...])
            up = up_ref[...] + dot(far_ref[...], up_w_ref[...])
            gate_ref[...] = gate
            up_ref[...] = up
            hidden_ref[...] = act_hidden(gate, up)

    whole = pl.BlockSpec((rows, hidden_units), lambda j, a_ref: (0, 0))
    weight = pl.BlockSpec((step, hidden_units), lambda j, a_ref: (2 * (1 - a_ref[0]) + j, 0))
    wide = jax.ShapeDtypeStruct((rows, hidden_units), F32)
    return pl.pallas_call(
        kernel,
        grid_spec=pltpu.PrefetchScalarGridSpec(
            num_scalar_prefetch=1,
            grid=(2,),
            in_specs=[
                pl.BlockSpec((rows, step), lambda j, a_ref: (0, j)),
                whole,
                whole,
                weight,
                weight,
            ],
            out_specs=[whole, whole, whole],
        ),
        out_shape=[wide, wide, jax.ShapeDtypeStruct((rows, hidden_units), BF)],
        name="forward_far",
    )(a, far, gate_near, up_near, gate_w, up_w)


def forward(a, near, far, gate_w, up_w):
    rows, half = near.shape
    hidden_units = gate_w.shape[1]
    step = half // 2

    def kernel(a_ref, near_ref, far_ref, gate_w_ref, up_w_ref, gate_ref, up_ref, hidden_ref):
        j = pl.program_id(0)

        @pl.when(j == 0)
        def _():
            gate_ref[...] = dot(near_ref[...], gate_w_ref[...])
            up_ref[...] = dot(near_ref[...], up_w_ref[...])

        @pl.when(j == 1)
        def _():
            gate_ref[...] += dot(near_ref[...], gate_w_ref[...])
            up_ref[...] += dot(near_ref[...], up_w_ref[...])

        @pl.when(j == 2)
        def _():
            gate_ref[...] += dot(far_ref[...], gate_w_ref[...])
            up_ref[...] += dot(far_ref[...], up_w_ref[...])

        @pl.when(j == 3)
        def _():
            gate = gate_ref[...] + dot(far_ref[...], gate_w_ref[...])
            up = up_ref[...] + dot(far_ref[...], up_w_ref[...])
            gate_ref[...] = gate
            up_ref[...] = up
            hidden_ref[...] = act_hidden(gate, up)

    whole = pl.BlockSpec((rows, hidden_units), lambda j, a_ref: (0, 0))
    weight = pl.BlockSpec((step, hidden_units), lambda j, a_ref: (near_first(j, a_ref[0]), 0))
    return pl.pallas_call(
        kernel,
        grid_spec=pltpu.PrefetchScalarGridSpec(
            num_scalar_prefetch=1,
            grid=(4,),
            in_specs=[
                pl.BlockSpec((rows, step), lambda j, a_ref: (0, jnp.minimum(j, 1))),
                pl.BlockSpec((rows, step), lambda j, a_ref: (0, jnp.maximum(j - 2, 0))),
                weight,
                weight,
            ],
            out_specs=[whole, whole, whole],
        ),
        out_shape=[
            jax.ShapeDtypeStruct((rows, hidden_units), F32),
            jax.ShapeDtypeStruct((rows, hidden_units), F32),
            jax.ShapeDtypeStruct((rows, hidden_units), BF),
        ],
        name="forward",
    )(a, near, far, gate_w, up_w)


def gradients(a, grad_rows, down, hidden_in, gate, up, gate_w, up_w, base, dtype):
    rows, half = grad_rows.shape
    hidden_units = gate_w.shape[1]
    step = half // 2

    def kernel(a_ref, c_ref, down_ref, in_ref, gate_ref, up_ref, gw_ref, uw_ref, *rest):
        base_ref = None if base is None else rest[0]
        gg_ref, ug_ref, out_ref = rest[-3:]

        @pl.when(pl.program_id(0) == 0)
        def _():
            hidden_grad = dot(c_ref[...], down_ref[...], 1, 1) + in_ref[...].astype(F32)
            gate = gate_ref[...]
            sig = jax.nn.sigmoid(gate)
            gg_ref[...] = (
                hidden_grad * up_ref[...] * sig * (1.0 + gate * (1.0 - sig))
            ).astype(BF)
            ug_ref[...] = (hidden_grad * (gate * sig)).astype(BF)

        value = dot(gg_ref[...], gw_ref[...], 1, 1) + dot(ug_ref[...], uw_ref[...], 1, 1)
        if base_ref is not None:
            value = value + base_ref[...]
        out_ref[...] = value.astype(dtype)

    def whole(x):
        return pl.BlockSpec(x.shape, lambda j, a_ref: (0, 0))

    weight = pl.BlockSpec((step, hidden_units), lambda j, a_ref: (2 * (1 - a_ref[0]) + j, 0))
    block = pl.BlockSpec((rows, step), lambda j, a_ref: (0, j))
    operands = [grad_rows, down, hidden_in, gate, up, gate_w, up_w]
    in_specs = [whole(x) for x in operands[:5]] + [weight, weight]
    if base is not None:
        operands.append(base)
        in_specs.append(block)
    grad = jax.ShapeDtypeStruct((rows, hidden_units), BF)
    return pl.pallas_call(
        kernel,
        grid_spec=pltpu.PrefetchScalarGridSpec(
            num_scalar_prefetch=1,
            grid=(2,),
            in_specs=in_specs,
            out_specs=[whole(grad), whole(grad), block],
        ),
        out_shape=[grad, grad, jax.ShapeDtypeStruct((rows, half), dtype)],
        name="gradients",
    )(a, *operands)


def layer(tokens, expert_ids, route_weights, w_gate, w_up, w_down, cotangent):
    num_experts = lax.axis_size("expert")
    tok_rows, top = expert_ids.shape
    capacity = tok_rows * top * 4 // (num_experts * 3)
    slots = capacity // 2
    y = lax.axis_index("replica")
    a = y >> 1
    b = ((y + 1) >> 1) & 1
    gate_w, up_w, down_w = w_gate[0], w_up[0], w_down[0]

    gate_b = swap_b(gate_w)
    up_b = swap_b(up_w)
    down_own, down_far = halves(down_w, 1, a)
    down_a = swap_a(down_far)
    down_ab = swap_b(down_a)
    down_b = swap_b(down_own)

    experts = jnp.arange(num_experts, dtype=jnp.int32)
    hit = expert_ids.T[None, :, :] == experts[:, None, None]
    chosen = jnp.sum(hit.astype(F32), axis=1)
    weight = jnp.sum(jnp.where(hit, route_weights.T[None, :, :], 0.0), axis=1)
    before = jnp.arange(tok_rows)[:, None] < jnp.arange(tok_rows)[None, :]
    rank = dot(chosen.astype(BF), before.astype(BF))
    place = jnp.where(chosen > 0, rank.astype(jnp.int32) - slots * b, -1)
    pick = place[:, None, :] == jnp.arange(slots, dtype=jnp.int32)[None, :, None]
    pick_w = jnp.where(pick, weight[:, None, :], 0.0).reshape(-1, tok_rows)
    pick = pick.astype(BF).reshape(-1, tok_rows)
    slot_weight = jnp.sum(pick_w, axis=1, keepdims=True)
    pick_hi = pick_w.astype(BF)
    pick_lo = (pick_w - pick_hi.astype(F32)).astype(BF)

    tok_half, _ = halves(tokens, 1, a)
    cot_half, _ = halves(cotangent, 1, a)
    packed = dot(pick, tok_half).astype(BF)
    rows_near = exchange(packed, num_experts)
    rows_far = swap_a(rows_near)
    packed_grad = (dot(pick, cot_half) * slot_weight).astype(BF)
    grad_rows = exchange(packed_grad, num_experts)

    at = a.reshape(1)
    gate_n, up_n = forward_near(at, rows_near, gate_w, up_w)
    gate_1, up_1, hidden_1 = forward_far(at, rows_far, gate_n, up_n, gate_w, up_w)
    gate_2, up_2, hidden_2 = forward(at, rows_near, rows_far, gate_b, up_b)
    hidden_3 = swap_a(hidden_1)
    hidden_4 = swap_a(hidden_2)
    hgrad_3 = dot(grad_rows, down_a, 1, 1).astype(BF)
    hgrad_3 = swap_a(hgrad_3)
    hgrad_4 = dot(grad_rows, down_ab, 1, 1).astype(BF)
    hgrad_4 = swap_a(hgrad_4)

    mixed_rows = dot(hidden_1, down_own) + dot(hidden_3, down_a)
    mixed_rows = lax.optimization_barrier(mixed_rows + dot(hidden_4, down_ab))
    mixed_rows = (mixed_rows + dot(hidden_2, down_b)).astype(BF)
    mixed_back = exchange(mixed_rows, num_experts)

    gg_1, ug_1, base = gradients(
        at, grad_rows, down_own, hgrad_3, gate_1, up_1, gate_w, up_w, None, F32
    )
    gg_2, ug_2, far = gradients(
        at, grad_rows, down_b, hgrad_4, gate_2, up_2, gate_b, up_b, base, BF
    )
    far = swap_a(far)
    gate_1n, _ = halves(gate_w, 0, a)
    up_1n, _ = halves(up_w, 0, a)
    gate_2n, _ = halves(gate_b, 0, a)
    up_2n, _ = halves(up_b, 0, a)
    near = dot(gg_1, gate_1n, 1, 1) + dot(ug_1, up_1n, 1, 1)
    near = near + dot(gg_2, gate_2n, 1, 1) + dot(ug_2, up_2n, 1, 1)
    near = lax.optimization_barrier(near)
    near = (near + far.astype(F32)).astype(BF)
    grad_back = exchange(near, num_experts)

    def finish(partial):
        keep, give = halves(partial, 1, y & 1)
        return (keep + swap_b(give.astype(BF)).astype(F32)).astype(BF)

    mixed = finish(dot(pick_hi, mixed_back, 0, 0) + dot(pick_lo, mixed_back, 0, 0))
    tokens_grad = finish(dot(pick, grad_back, 0, 0))
    return (mixed, tokens_grad)


def solution(mesh):
    in_specs = (
        P("expert", None),
        P("expert", None),
        P("expert", None),
        P("expert", None, "replica"),
        P("expert", None, "replica"),
        P("expert", "replica", None),
        P("expert", None),
    )
    out_specs = (P("expert", "replica"), P("expert", "replica"))
    return jax.shard_map(layer, mesh=mesh, in_specs=in_specs, out_specs=out_specs, check_vma=False)
```

```python
import jax
import jax.numpy as jnp
from jax import lax
from jax.experimental import pallas as pl
from jax.experimental.pallas import tpu as pltpu
from jax.sharding import PartitionSpec as P


BF = jnp.bfloat16
F32 = jnp.float32
PAIRS_0 = (1, 0, 3, 2)
PAIRS_1 = (3, 2, 1, 0)


def swap(value, even, odd):
    pairs = []
    for expert in range(lax.axis_size("expert")):
        partner = odd if expert % 2 else even
        pairs += [(expert * 4 + y, expert * 4 + partner[y]) for y in range(4)]
    return lax.ppermute(value, ("expert", "replica"), pairs)


def swap_b(value):
    return swap(value, PAIRS_0, PAIRS_1)


def swap_a(value):
    return swap(value, PAIRS_1, PAIRS_0)


def dot(lhs, rhs, ldim=1, rdim=0):
    return lax.dot_general(lhs, rhs, (((ldim,), (rdim,)), ((), ())), preferred_element_type=F32)


def choose(value, index):
    quarters = jnp.split(value, 4, axis=1)
    low = jnp.where(index == 0, quarters[0], quarters[1])
    high = jnp.where(index == 2, quarters[2], quarters[3])
    return jnp.where(index < 2, low, high)


def columns(value, first, second):
    return jnp.concatenate([choose(value, first), choose(value, second)], axis=1)


def rows_of(value, first, second):
    size = value.shape[0] // 4
    return jnp.concatenate(
        [
            lax.dynamic_slice_in_dim(value, first * size, size, 0),
            lax.dynamic_slice_in_dim(value, second * size, size, 0),
        ],
        axis=0,
    )


def exchange(rows, num_experts):
    width = rows.shape[1]
    moved = lax.all_to_all(
        rows.reshape(num_experts, -1, width), "expert", split_axis=0, concat_axis=0, tiled=True
    )
    return moved.reshape(-1, width)


def act_hidden(gate, up):
    return (gate * jax.nn.sigmoid(gate) * up).astype(BF)


def forward_near(order, near, gate_w, up_w):
    rows, half = near.shape
    hidden_units = gate_w.shape[1]
    step = half // 2

    def kernel(order_ref, near_ref, gate_w_ref, up_w_ref, gate_ref, up_ref):
        gate = dot(near_ref[...], gate_w_ref[...])
        up = dot(near_ref[...], up_w_ref[...])

        @pl.when(pl.program_id(0) == 0)
        def _():
            gate_ref[...] = gate
            up_ref[...] = up

        @pl.when(pl.program_id(0) == 1)
        def _():
            gate_ref[...] += gate
            up_ref[...] += up

    whole = pl.BlockSpec((rows, hidden_units), lambda j, order_ref: (0, 0))
    weight = pl.BlockSpec((step, hidden_units), lambda j, order_ref: (order_ref[j], 0))
    return pl.pallas_call(
        kernel,
        grid_spec=pltpu.PrefetchScalarGridSpec(
            num_scalar_prefetch=1,
            grid=(2,),
            in_specs=[pl.BlockSpec((rows, step), lambda j, order_ref: (0, j)), weight, weight],
            out_specs=[whole, whole],
        ),
        out_shape=[jax.ShapeDtypeStruct((rows, hidden_units), F32)] * 2,
        name="forward_near",
    )(order, near, gate_w, up_w)


def forward_far(order, far, gate_near, up_near, gate_w, up_w):
    rows, half = far.shape
    hidden_units = gate_w.shape[1]
    step = half // 2

    def kernel(order_ref, far_ref, gn_ref, un_ref, gate_w_ref, up_w_ref, gate_ref, up_ref, hidden_ref):
        @pl.when(pl.program_id(0) == 0)
        def _():
            gate_ref[...] = gn_ref[...] + dot(far_ref[...], gate_w_ref[...])
            up_ref[...] = un_ref[...] + dot(far_ref[...], up_w_ref[...])

        @pl.when(pl.program_id(0) == 1)
        def _():
            gate = gate_ref[...] + dot(far_ref[...], gate_w_ref[...])
            up = up_ref[...] + dot(far_ref[...], up_w_ref[...])
            gate_ref[...] = gate
            up_ref[...] = up
            hidden_ref[...] = act_hidden(gate, up)

    whole = pl.BlockSpec((rows, hidden_units), lambda j, order_ref: (0, 0))
    weight = pl.BlockSpec((step, hidden_units), lambda j, order_ref: (order_ref[2 + j], 0))
    wide = jax.ShapeDtypeStruct((rows, hidden_units), F32)
    return pl.pallas_call(
        kernel,
        grid_spec=pltpu.PrefetchScalarGridSpec(
            num_scalar_prefetch=1,
            grid=(2,),
            in_specs=[
                pl.BlockSpec((rows, step), lambda j, order_ref: (0, j)),
                whole,
                whole,
                weight,
                weight,
            ],
            out_specs=[whole, whole, whole],
        ),
        out_shape=[wide, wide, jax.ShapeDtypeStruct((rows, hidden_units), BF)],
        name="forward_far",
    )(order, far, gate_near, up_near, gate_w, up_w)


def forward(order, near, far, gate_w, up_w):
    rows, half = near.shape
    hidden_units = gate_w.shape[1]
    step = half // 2

    def kernel(order_ref, near_ref, far_ref, gate_w_ref, up_w_ref, gate_ref, up_ref, hidden_ref):
        j = pl.program_id(0)

        @pl.when(j == 0)
        def _():
            gate_ref[...] = dot(near_ref[...], gate_w_ref[...])
            up_ref[...] = dot(near_ref[...], up_w_ref[...])

        @pl.when(j == 1)
        def _():
            gate_ref[...] += dot(near_ref[...], gate_w_ref[...])
            up_ref[...] += dot(near_ref[...], up_w_ref[...])

        @pl.when(j == 2)
        def _():
            gate_ref[...] += dot(far_ref[...], gate_w_ref[...])
            up_ref[...] += dot(far_ref[...], up_w_ref[...])

        @pl.when(j == 3)
        def _():
            gate = gate_ref[...] + dot(far_ref[...], gate_w_ref[...])
            up = up_ref[...] + dot(far_ref[...], up_w_ref[...])
            gate_ref[...] = gate
            up_ref[...] = up
            hidden_ref[...] = act_hidden(gate, up)

    whole = pl.BlockSpec((rows, hidden_units), lambda j, order_ref: (0, 0))
    weight = pl.BlockSpec((step, hidden_units), lambda j, order_ref: (order_ref[j], 0))
    return pl.pallas_call(
        kernel,
        grid_spec=pltpu.PrefetchScalarGridSpec(
            num_scalar_prefetch=1,
            grid=(4,),
            in_specs=[
                pl.BlockSpec((rows, step), lambda j, order_ref: (0, jnp.minimum(j, 1))),
                pl.BlockSpec((rows, step), lambda j, order_ref: (0, jnp.maximum(j - 2, 0))),
                weight,
                weight,
            ],
            out_specs=[whole, whole, whole],
        ),
        out_shape=[
            jax.ShapeDtypeStruct((rows, hidden_units), F32),
            jax.ShapeDtypeStruct((rows, hidden_units), F32),
            jax.ShapeDtypeStruct((rows, hidden_units), BF),
        ],
        name="forward",
    )(order, near, far, gate_w, up_w)


def gradients(order, grad_rows, down, hidden_in, gate, up, gate_w, up_w, base, dtype):
    rows, half = grad_rows.shape
    hidden_units = gate_w.shape[1]
    step = half // 2

    def kernel(order_ref, c_ref, down_ref, in_ref, gate_ref, up_ref, gw_ref, uw_ref, *rest):
        base_ref = None if base is None else rest[0]
        gg_ref, ug_ref, out_ref = rest[-3:]

        @pl.when(pl.program_id(0) == 0)
        def _():
            hidden_grad = dot(c_ref[...], down_ref[...], 1, 1) + in_ref[...].astype(F32)
            gate = gate_ref[...]
            sig = jax.nn.sigmoid(gate)
            gg_ref[...] = (
                hidden_grad * up_ref[...] * sig * (1.0 + gate * (1.0 - sig))
            ).astype(BF)
            ug_ref[...] = (hidden_grad * (gate * sig)).astype(BF)

        value = dot(gg_ref[...], gw_ref[...], 1, 1) + dot(ug_ref[...], uw_ref[...], 1, 1)
        if base_ref is not None:
            value = value + base_ref[...]
        out_ref[...] = value.astype(dtype)

    def whole(x):
        return pl.BlockSpec(x.shape, lambda j, order_ref: (0, 0))

    weight = pl.BlockSpec((step, hidden_units), lambda j, order_ref: (order_ref[2 + j], 0))
    block = pl.BlockSpec((rows, step), lambda j, order_ref: (0, j))
    operands = [grad_rows, down, hidden_in, gate, up, gate_w, up_w]
    in_specs = [whole(x) for x in operands[:5]] + [weight, weight]
    if base is not None:
        operands.append(base)
        in_specs.append(block)
    grad = jax.ShapeDtypeStruct((rows, hidden_units), BF)
    return pl.pallas_call(
        kernel,
        grid_spec=pltpu.PrefetchScalarGridSpec(
            num_scalar_prefetch=1,
            grid=(2,),
            in_specs=in_specs,
            out_specs=[whole(grad), whole(grad), block],
        ),
        out_shape=[grad, grad, jax.ShapeDtypeStruct((rows, half), dtype)],
        name="gradients",
    )(order, *operands)


def layer(tokens, expert_ids, route_weights, w_gate, w_up, w_down, cotangent):
    num_experts = lax.axis_size("expert")
    tok_rows, top = expert_ids.shape
    capacity = tok_rows * top * 4 // (num_experts * 3)
    slots = capacity // 2
    y = lax.axis_index("replica")
    odd = lax.axis_index("expert") & 1
    outer = y >> 1
    inner = ((y + 1) >> 1) & 1
    near_0 = jnp.where(odd == 0, 2 * outer, inner)
    near_1 = jnp.where(odd == 0, 2 * outer + 1, 3 - inner)
    far_0 = jnp.where(odd == 0, 2 - 2 * outer, 1 - inner)
    far_1 = jnp.where(odd == 0, 3 - 2 * outer, 2 + inner)
    order = jnp.stack([near_0, near_1, far_0, far_1])
    gate_w, up_w, down_w = w_gate[0], w_up[0], w_down[0]

    gate_b = swap_b(gate_w)
    up_b = swap_b(up_w)
    down_own = columns(down_w, near_0, near_1)
    down_far = columns(down_w, far_0, far_1)
    down_a = swap_a(down_far)
    down_ab = swap_b(down_a)
    down_b = swap_b(down_own)

    experts = jnp.arange(num_experts, dtype=jnp.int32)
    hit = expert_ids.T[None, :, :] == experts[:, None, None]
    chosen = jnp.sum(hit.astype(F32), axis=1)
    weight = jnp.sum(jnp.where(hit, route_weights.T[None, :, :], 0.0), axis=1)
    before = jnp.arange(tok_rows)[:, None] < jnp.arange(tok_rows)[None, :]
    rank = dot(chosen.astype(BF), before.astype(BF))
    is_odd = (experts & 1)[:, None] == 1
    first_slot = slots * jnp.where(is_odd, outer, inner)
    place = jnp.where(chosen > 0, rank.astype(jnp.int32) - first_slot, -1)
    pick = place[:, None, :] == jnp.arange(slots, dtype=jnp.int32)[None, :, None]
    pick_w = jnp.where(pick, weight[:, None, :], 0.0)
    slot_weight = jnp.sum(pick_w, axis=2).reshape(-1, 1)
    is_odd = is_odd[:, :, None]

    def by_parity(value):
        parts = [jnp.where(is_odd, 0, value), jnp.where(is_odd, value, 0)]
        return jnp.concatenate(parts, axis=2).reshape(-1, 2 * tok_rows)

    pick = by_parity(pick.astype(BF))
    pick_hi = pick_w.astype(BF)
    pick_lo = by_parity((pick_w - pick_hi.astype(F32)).astype(BF))
    pick_hi = by_parity(pick_hi)

    def both(value):
        even = columns(value, 2 * outer, 2 * outer + 1)
        return jnp.concatenate([even, columns(value, inner, 3 - inner)], axis=0)

    packed = dot(pick, both(tokens)).astype(BF)
    rows_near = exchange(packed, num_experts)
    rows_far = swap_a(rows_near)
    packed_grad = (dot(pick, both(cotangent)) * slot_weight).astype(BF)
    grad_rows = exchange(packed_grad, num_experts)

    gate_n, up_n = forward_near(order, rows_near, gate_w, up_w)
    gate_1, up_1, hidden_1 = forward_far(order, rows_far, gate_n, up_n, gate_w, up_w)
    gate_2, up_2, hidden_2 = forward(order, rows_near, rows_far, gate_b, up_b)
    hidden_3 = swap_a(hidden_1)
    hidden_4 = swap_a(hidden_2)
    hgrad_3 = dot(grad_rows, down_a, 1, 1).astype(BF)
    hgrad_3 = swap_a(hgrad_3)
    hgrad_4 = dot(grad_rows, down_ab, 1, 1).astype(BF)
    hgrad_4 = swap_a(hgrad_4)

    mixed_rows = dot(hidden_1, down_own) + dot(hidden_3, down_a)
    mixed_rows = lax.optimization_barrier(mixed_rows + dot(hidden_4, down_ab))
    mixed_rows = (mixed_rows + dot(hidden_2, down_b)).astype(BF)
    mixed_back = exchange(mixed_rows, num_experts)

    gg_1, ug_1, base = gradients(
        order, grad_rows, down_own, hgrad_3, gate_1, up_1, gate_w, up_w, None, F32
    )
    gg_2, ug_2, far = gradients(
        order, grad_rows, down_b, hgrad_4, gate_2, up_2, gate_b, up_b, base, BF
    )
    far = swap_a(far)
    gate_1n = rows_of(gate_w, near_0, near_1)
    up_1n = rows_of(up_w, near_0, near_1)
    gate_2n = rows_of(gate_b, near_0, near_1)
    up_2n = rows_of(up_b, near_0, near_1)
    near = dot(gg_1, gate_1n, 1, 1) + dot(ug_1, up_1n, 1, 1)
    near = near + dot(gg_2, gate_2n, 1, 1) + dot(ug_2, up_2n, 1, 1)
    near = lax.optimization_barrier(near)
    near = (near + far.astype(F32)).astype(BF)
    grad_back = exchange(near, num_experts)

    def finish(partial):
        def share(value, at, pairs):
            low, high = jnp.split(value, 2, axis=1)
            keep = jnp.where(at == 0, low, high)
            give = jnp.where(at == 0, high, low).astype(BF)
            return keep + lax.ppermute(give, "replica", list(enumerate(pairs))).astype(F32)

        even, odd_part = jnp.split(partial, 2, axis=0)
        total = share(even, y & 1, PAIRS_0) + share(odd_part, outer, PAIRS_1)
        return total.astype(BF)

    mixed = finish(dot(pick_hi, mixed_back, 0, 0) + dot(pick_lo, mixed_back, 0, 0))
    tokens_grad = finish(dot(pick, grad_back, 0, 0))
    return (mixed, tokens_grad)


def solution(mesh):
    in_specs = (
        P("expert", None),
        P("expert", None),
        P("expert", None),
        P("expert", None, "replica"),
        P("expert", None, "replica"),
        P("expert", "replica", None),
        P("expert", None),
    )
    out_specs = (P("expert", "replica"), P("expert", "replica"))
    return jax.shard_map(layer, mesh=mesh, in_specs=in_specs, out_specs=out_specs, check_vma=False)
```

```python
import jax
import jax.numpy as jnp
from jax import lax
from jax.experimental import pallas as pl
from jax.experimental.pallas import tpu as pltpu
from jax.sharding import PartitionSpec as P


BF = jnp.bfloat16
F32 = jnp.float32
PAIRS_0 = (1, 0, 3, 2)
PAIRS_1 = (3, 2, 1, 0)


def swap(value, even, odd):
    pairs = []
    for expert in range(lax.axis_size("expert")):
        partner = odd if expert % 2 else even
        pairs += [(expert * 4 + y, expert * 4 + partner[y]) for y in range(4)]
    return lax.ppermute(value, ("expert", "replica"), pairs)


def swap_b(value):
    return swap(value, PAIRS_0, PAIRS_1)


def swap_a(value):
    return swap(value, PAIRS_1, PAIRS_0)


def dot(lhs, rhs, ldim=1, rdim=0):
    return lax.dot_general(lhs, rhs, (((ldim,), (rdim,)), ((), ())), preferred_element_type=F32)


def choose(value, index):
    quarters = jnp.split(value, 4, axis=1)
    low = jnp.where(index == 0, quarters[0], quarters[1])
    high = jnp.where(index == 2, quarters[2], quarters[3])
    return jnp.where(index < 2, low, high)


def columns(value, first, second):
    return jnp.concatenate([choose(value, first), choose(value, second)], axis=1)


def rows_of(value, first, second):
    size = value.shape[0] // 4
    return jnp.concatenate(
        [
            lax.dynamic_slice_in_dim(value, first * size, size, 0),
            lax.dynamic_slice_in_dim(value, second * size, size, 0),
        ],
        axis=0,
    )


def exchange(rows, num_experts):
    width = rows.shape[1]
    moved = lax.all_to_all(
        rows.reshape(num_experts, -1, width), "expert", split_axis=0, concat_axis=0, tiled=True
    )
    return moved.reshape(-1, width)


def act_hidden(gate, up):
    return (gate * jax.nn.sigmoid(gate) * up).astype(BF)


def forward_near(order, near, gate_w, up_w):
    rows, half = near.shape
    hidden_units = gate_w.shape[1]
    step = half // 2

    def kernel(order_ref, near_ref, gate_w_ref, up_w_ref, gate_ref, up_ref):
        gate = dot(near_ref[...], gate_w_ref[...])
        up = dot(near_ref[...], up_w_ref[...])

        @pl.when(pl.program_id(0) == 0)
        def _():
            gate_ref[...] = gate
            up_ref[...] = up

        @pl.when(pl.program_id(0) == 1)
        def _():
            gate_ref[...] += gate
            up_ref[...] += up

    whole = pl.BlockSpec((rows, hidden_units), lambda j, order_ref: (0, 0))
    weight = pl.BlockSpec((step, hidden_units), lambda j, order_ref: (order_ref[j], 0))
    return pl.pallas_call(
        kernel,
        grid_spec=pltpu.PrefetchScalarGridSpec(
            num_scalar_prefetch=1,
            grid=(2,),
            in_specs=[pl.BlockSpec((rows, step), lambda j, order_ref: (0, j)), weight, weight],
            out_specs=[whole, whole],
        ),
        out_shape=[jax.ShapeDtypeStruct((rows, hidden_units), F32)] * 2,
        name="forward_near",
    )(order, near, gate_w, up_w)


def forward_far(order, far, gate_near, up_near, gate_w, up_w):
    rows, half = far.shape
    hidden_units = gate_w.shape[1]
    step = half // 2

    def kernel(order_ref, far_ref, gn_ref, un_ref, gate_w_ref, up_w_ref, gate_ref, up_ref, hidden_ref):
        @pl.when(pl.program_id(0) == 0)
        def _():
            gate_ref[...] = gn_ref[...] + dot(far_ref[...], gate_w_ref[...])
            up_ref[...] = un_ref[...] + dot(far_ref[...], up_w_ref[...])

        @pl.when(pl.program_id(0) == 1)
        def _():
            gate = gate_ref[...] + dot(far_ref[...], gate_w_ref[...])
            up = up_ref[...] + dot(far_ref[...], up_w_ref[...])
            gate_ref[...] = gate
            up_ref[...] = up
            hidden_ref[...] = act_hidden(gate, up)

    whole = pl.BlockSpec((rows, hidden_units), lambda j, order_ref: (0, 0))
    weight = pl.BlockSpec((step, hidden_units), lambda j, order_ref: (order_ref[2 + j], 0))
    wide = jax.ShapeDtypeStruct((rows, hidden_units), F32)
    return pl.pallas_call(
        kernel,
        grid_spec=pltpu.PrefetchScalarGridSpec(
            num_scalar_prefetch=1,
            grid=(2,),
            in_specs=[
                pl.BlockSpec((rows, step), lambda j, order_ref: (0, j)),
                whole,
                whole,
                weight,
                weight,
            ],
            out_specs=[whole, whole, whole],
        ),
        out_shape=[wide, wide, jax.ShapeDtypeStruct((rows, hidden_units), BF)],
        name="forward_far",
    )(order, far, gate_near, up_near, gate_w, up_w)


def forward(order, near, far, gate_w, up_w):
    rows, half = near.shape
    hidden_units = gate_w.shape[1]
    step = half // 2

    def kernel(order_ref, near_ref, far_ref, gate_w_ref, up_w_ref, gate_ref, up_ref, hidden_ref):
        j = pl.program_id(0)

        @pl.when(j == 0)
        def _():
            gate_ref[...] = dot(near_ref[...], gate_w_ref[...])
            up_ref[...] = dot(near_ref[...], up_w_ref[...])

        @pl.when(j == 1)
        def _():
            gate_ref[...] += dot(near_ref[...], gate_w_ref[...])
            up_ref[...] += dot(near_ref[...], up_w_ref[...])

        @pl.when(j == 2)
        def _():
            gate_ref[...] += dot(far_ref[...], gate_w_ref[...])
            up_ref[...] += dot(far_ref[...], up_w_ref[...])

        @pl.when(j == 3)
        def _():
            gate = gate_ref[...] + dot(far_ref[...], gate_w_ref[...])
            up = up_ref[...] + dot(far_ref[...], up_w_ref[...])
            gate_ref[...] = gate
            up_ref[...] = up
            hidden_ref[...] = act_hidden(gate, up)

    whole = pl.BlockSpec((rows, hidden_units), lambda j, order_ref: (0, 0))
    weight = pl.BlockSpec((step, hidden_units), lambda j, order_ref: (order_ref[j], 0))
    return pl.pallas_call(
        kernel,
        grid_spec=pltpu.PrefetchScalarGridSpec(
            num_scalar_prefetch=1,
            grid=(4,),
            in_specs=[
                pl.BlockSpec((rows, step), lambda j, order_ref: (0, jnp.minimum(j, 1))),
                pl.BlockSpec((rows, step), lambda j, order_ref: (0, jnp.maximum(j - 2, 0))),
                weight,
                weight,
            ],
            out_specs=[whole, whole, whole],
        ),
        out_shape=[
            jax.ShapeDtypeStruct((rows, hidden_units), F32),
            jax.ShapeDtypeStruct((rows, hidden_units), F32),
            jax.ShapeDtypeStruct((rows, hidden_units), BF),
        ],
        name="forward",
    )(order, near, far, gate_w, up_w)


def gradients(order, grad_rows, first, second):
    rows, half = grad_rows.shape
    hidden_units = first[2].shape[1]
    step = half // 2

    def kernel(order_ref, c_hbm, *refs):
        sources, outs = (refs[:6], refs[6:12]), refs[12:17]
        far_ref = outs[4]
        c_ref, scratch, sem = refs[17], (refs[18:24], refs[24:30]), refs[30]
        copies = []

        def start(source, target):
            copy = pltpu.make_async_copy(source, target, sem.at[len(copies)])
            copy.start()
            copies.append(copy)
            return copy

        c_copy = start(c_hbm, c_ref)
        small = [[start(sources[s][k], scratch[s][k]) for k in range(4)] for s in range(2)]
        large = [
            [
                start(
                    sources[s][4 + k].at[pl.ds(order_ref[2 + n] * step, step), :],
                    scratch[s][4 + k].at[pl.ds(n * step, step), :],
                )
                for s in range(2)
                for k in range(2)
            ]
            for n in range(2)
        ]
        c_copy.wait()
        for s in range(2):
            down_ref, in_ref, gate_ref, up_ref = scratch[s][:4]
            gg_ref, ug_ref = outs[2 * s], outs[2 * s + 1]
            small[s][0].wait()
            hidden_grad = dot(c_ref[...], down_ref[...], 1, 1)
            for copy in small[s][1:]:
                copy.wait()
            hidden_grad = hidden_grad + in_ref[...].astype(F32)
            gate = gate_ref[...]
            sig = jax.nn.sigmoid(gate)
            up_part = up_ref[...] * sig * (1.0 + gate * (1.0 - sig))
            gg_ref[...] = (hidden_grad * up_part).astype(BF)
            ug_ref[...] = (hidden_grad * (gate * sig)).astype(BF)
        for n in range(2):
            for copy in large[n]:
                copy.wait()
            block = pl.ds(n * step, step)
            value = dot(outs[0][...], scratch[0][4][block, :], 1, 1)
            value += dot(outs[1][...], scratch[0][5][block, :], 1, 1)
            value += dot(outs[2][...], scratch[1][4][block, :], 1, 1)
            value += dot(outs[3][...], scratch[1][5][block, :], 1, 1)
            far_ref[:, n * step : (n + 1) * step] = value.astype(BF)

    wide = pltpu.VMEM((rows, hidden_units), F32)
    weight = pltpu.VMEM((half, hidden_units), BF)
    one_slice = [
        pltpu.VMEM((hidden_units, half), BF),
        pltpu.VMEM((rows, hidden_units), BF),
        wide,
        wide,
        weight,
        weight,
    ]
    anywhere = pl.BlockSpec(memory_space=pl.ANY)
    grad = jax.ShapeDtypeStruct((rows, hidden_units), BF)
    return pl.pallas_call(
        kernel,
        in_specs=[pl.BlockSpec(memory_space=pltpu.SMEM)] + [anywhere] * 13,
        out_shape=[grad, grad, grad, grad, jax.ShapeDtypeStruct((rows, half), BF)],
        scratch_shapes=[
            pltpu.VMEM((rows, half), BF),
            *one_slice,
            *one_slice,
            pltpu.SemaphoreType.DMA((17,)),
        ],
        name="gradients",
    )(order, grad_rows, *first, *second)


def layer(tokens, expert_ids, route_weights, w_gate, w_up, w_down, cotangent):
    num_experts = lax.axis_size("expert")
    tok_rows, top = expert_ids.shape
    capacity = tok_rows * top * 4 // (num_experts * 3)
    slots = capacity // 2
    y = lax.axis_index("replica")
    odd = lax.axis_index("expert") & 1
    outer = y >> 1
    inner = ((y + 1) >> 1) & 1
    near_0 = jnp.where(odd == 0, 2 * outer, inner)
    near_1 = jnp.where(odd == 0, 2 * outer + 1, 3 - inner)
    far_0 = jnp.where(odd == 0, 2 - 2 * outer, 1 - inner)
    far_1 = jnp.where(odd == 0, 3 - 2 * outer, 2 + inner)
    order = jnp.stack([near_0, near_1, far_0, far_1])
    gate_w, up_w, down_w = w_gate[0], w_up[0], w_down[0]

    gate_b = swap_b(gate_w)
    up_b = swap_b(up_w)
    down_own = columns(down_w, near_0, near_1)
    down_far = columns(down_w, far_0, far_1)
    down_a = swap_a(down_far)
    down_ab = swap_b(down_a)
    down_b = swap_b(down_own)

    experts = jnp.arange(num_experts, dtype=jnp.int32)
    hit = expert_ids.T[None, :, :] == experts[:, None, None]
    chosen = jnp.sum(hit.astype(F32), axis=1)
    weight = jnp.sum(jnp.where(hit, route_weights.T[None, :, :], 0.0), axis=1)
    before = jnp.arange(tok_rows)[:, None] < jnp.arange(tok_rows)[None, :]
    rank = dot(chosen.astype(BF), before.astype(BF))
    is_odd = (experts & 1)[:, None] == 1
    first_slot = slots * jnp.where(is_odd, outer, inner)
    place = jnp.where(chosen > 0, rank.astype(jnp.int32) - first_slot, -1)
    pick = place[:, None, :] == jnp.arange(slots, dtype=jnp.int32)[None, :, None]
    pick_w = jnp.where(pick, weight[:, None, :], 0.0)
    slot_weight = jnp.sum(pick_w, axis=2).reshape(-1, 1)
    is_odd = is_odd[:, :, None]

    def by_parity(value):
        parts = [jnp.where(is_odd, 0, value), jnp.where(is_odd, value, 0)]
        return jnp.concatenate(parts, axis=2).reshape(-1, 2 * tok_rows)

    pick = by_parity(pick.astype(BF))
    pick_hi = pick_w.astype(BF)
    pick_lo = by_parity((pick_w - pick_hi.astype(F32)).astype(BF))
    pick_hi = by_parity(pick_hi)

    def both(value):
        even = columns(value, 2 * outer, 2 * outer + 1)
        return jnp.concatenate([even, columns(value, inner, 3 - inner)], axis=0)

    packed = dot(pick, both(tokens)).astype(BF)
    rows_near = exchange(packed, num_experts)
    rows_far = swap_a(rows_near)
    packed_grad = (dot(pick, both(cotangent)) * slot_weight).astype(BF)
    grad_rows = exchange(packed_grad, num_experts)

    gate_n, up_n = forward_near(order, rows_near, gate_w, up_w)
    gate_1, up_1, hidden_1 = forward_far(order, rows_far, gate_n, up_n, gate_w, up_w)
    gate_2, up_2, hidden_2 = forward(order, rows_near, rows_far, gate_b, up_b)
    hidden_3 = swap_a(hidden_1)
    hidden_4 = swap_a(hidden_2)
    hgrad_3 = dot(grad_rows, down_a, 1, 1).astype(BF)
    hgrad_3 = swap_a(hgrad_3)
    hgrad_4 = dot(grad_rows, down_ab, 1, 1).astype(BF)
    hgrad_4 = swap_a(hgrad_4)

    mixed_rows = dot(hidden_1, down_own) + dot(hidden_3, down_a)
    mixed_rows = lax.optimization_barrier(mixed_rows + dot(hidden_4, down_ab))
    mixed_rows = (mixed_rows + dot(hidden_2, down_b)).astype(BF)
    mixed_back = exchange(mixed_rows, num_experts)

    gg_1, ug_1, gg_2, ug_2, far = gradients(
        order,
        grad_rows,
        (down_own, hgrad_3, gate_1, up_1, gate_w, up_w),
        (down_b, hgrad_4, gate_2, up_2, gate_b, up_b),
    )
    far = swap_a(far)
    gate_1n = rows_of(gate_w, near_0, near_1)
    up_1n = rows_of(up_w, near_0, near_1)
    gate_2n = rows_of(gate_b, near_0, near_1)
    up_2n = rows_of(up_b, near_0, near_1)
    near = dot(gg_1, gate_1n, 1, 1) + dot(ug_1, up_1n, 1, 1)
    near = near + dot(gg_2, gate_2n, 1, 1) + dot(ug_2, up_2n, 1, 1)
    near = lax.optimization_barrier(near)
    near = (near + far.astype(F32)).astype(BF)
    grad_back = exchange(near, num_experts)

    def finish(partial):
        def share(value, at, pairs):
            low, high = jnp.split(value, 2, axis=1)
            keep = jnp.where(at == 0, low, high)
            give = jnp.where(at == 0, high, low).astype(BF)
            return keep + lax.ppermute(give, "replica", list(enumerate(pairs))).astype(F32)

        even, odd_part = jnp.split(partial, 2, axis=0)
        total = share(even, y & 1, PAIRS_0) + share(odd_part, outer, PAIRS_1)
        return total.astype(BF)

    mixed = finish(dot(pick_hi, mixed_back, 0, 0) + dot(pick_lo, mixed_back, 0, 0))
    tokens_grad = finish(dot(pick, grad_back, 0, 0))
    return (mixed, tokens_grad)


def solution(mesh):
    in_specs = (
        P("expert", None),
        P("expert", None),
        P("expert", None),
        P("expert", None, "replica"),
        P("expert", None, "replica"),
        P("expert", "replica", None),
        P("expert", None),
    )
    out_specs = (P("expert", "replica"), P("expert", "replica"))
    return jax.shard_map(layer, mesh=mesh, in_specs=in_specs, out_specs=out_specs, check_vma=False)
```

```python
import jax
import jax.numpy as jnp
from jax import lax
from jax.experimental import pallas as pl
from jax.experimental.pallas import tpu as pltpu
from jax.sharding import PartitionSpec as P


BF = jnp.bfloat16
F32 = jnp.float32
PAIRS_0 = (1, 0, 3, 2)
PAIRS_1 = (3, 2, 1, 0)


def swap(value, even, odd):
    pairs = []
    for expert in range(lax.axis_size("expert")):
        partner = odd if expert % 2 else even
        pairs += [(expert * 4 + y, expert * 4 + partner[y]) for y in range(4)]
    return lax.ppermute(value, ("expert", "replica"), pairs)


def swap_b(value):
    return swap(value, PAIRS_0, PAIRS_1)


def swap_a(value):
    return swap(value, PAIRS_1, PAIRS_0)


def dot(lhs, rhs, ldim=1, rdim=0):
    return lax.dot_general(lhs, rhs, (((ldim,), (rdim,)), ((), ())), preferred_element_type=F32)


def choose(value, index):
    quarters = jnp.split(value, 4, axis=1)
    low = jnp.where(index == 0, quarters[0], quarters[1])
    high = jnp.where(index == 2, quarters[2], quarters[3])
    return jnp.where(index < 2, low, high)


def columns(value, first, second):
    return jnp.concatenate([choose(value, first), choose(value, second)], axis=1)


def rows_of(value, first, second):
    size = value.shape[0] // 4
    return jnp.concatenate(
        [
            lax.dynamic_slice_in_dim(value, first * size, size, 0),
            lax.dynamic_slice_in_dim(value, second * size, size, 0),
        ],
        axis=0,
    )


def exchange(rows, num_experts):
    width = rows.shape[1]
    moved = lax.all_to_all(
        rows.reshape(num_experts, -1, width), "expert", split_axis=0, concat_axis=0, tiled=True
    )
    return moved.reshape(-1, width)


def act_hidden(gate, up):
    return (gate * jax.nn.sigmoid(gate) * up).astype(BF)


def forward_near(order, near, gate_w, up_w):
    rows, half = near.shape
    hidden_units = gate_w.shape[1]
    step = half // 2

    def kernel(order_ref, near_ref, gate_w_ref, up_w_ref, gate_ref, up_ref):
        gate = dot(near_ref[...], gate_w_ref[...])
        up = dot(near_ref[...], up_w_ref[...])

        @pl.when(pl.program_id(0) == 0)
        def _():
            gate_ref[...] = gate
            up_ref[...] = up

        @pl.when(pl.program_id(0) == 1)
        def _():
            gate_ref[...] += gate
            up_ref[...] += up

    whole = pl.BlockSpec((rows, hidden_units), lambda j, order_ref: (0, 0))
    weight = pl.BlockSpec((step, hidden_units), lambda j, order_ref: (order_ref[j], 0))
    return pl.pallas_call(
        kernel,
        grid_spec=pltpu.PrefetchScalarGridSpec(
            num_scalar_prefetch=1,
            grid=(2,),
            in_specs=[pl.BlockSpec((rows, step), lambda j, order_ref: (0, j)), weight, weight],
            out_specs=[whole, whole],
        ),
        out_shape=[jax.ShapeDtypeStruct((rows, hidden_units), F32)] * 2,
        name="forward_near",
    )(order, near, gate_w, up_w)


def forward_far(order, far, gate_near, up_near, gate_w, up_w):
    rows, half = far.shape
    hidden_units = gate_w.shape[1]
    step = half // 2

    def kernel(order_ref, far_ref, gn_ref, un_ref, gate_w_ref, up_w_ref, gate_ref, up_ref, hidden_ref):
        @pl.when(pl.program_id(0) == 0)
        def _():
            gate_ref[...] = gn_ref[...] + dot(far_ref[...], gate_w_ref[...])
            up_ref[...] = un_ref[...] + dot(far_ref[...], up_w_ref[...])

        @pl.when(pl.program_id(0) == 1)
        def _():
            gate = gate_ref[...] + dot(far_ref[...], gate_w_ref[...])
            up = up_ref[...] + dot(far_ref[...], up_w_ref[...])
            gate_ref[...] = gate
            up_ref[...] = up
            hidden_ref[...] = act_hidden(gate, up)

    whole = pl.BlockSpec((rows, hidden_units), lambda j, order_ref: (0, 0))
    weight = pl.BlockSpec((step, hidden_units), lambda j, order_ref: (order_ref[2 + j], 0))
    wide = jax.ShapeDtypeStruct((rows, hidden_units), F32)
    return pl.pallas_call(
        kernel,
        grid_spec=pltpu.PrefetchScalarGridSpec(
            num_scalar_prefetch=1,
            grid=(2,),
            in_specs=[
                pl.BlockSpec((rows, step), lambda j, order_ref: (0, j)),
                whole,
                whole,
                weight,
                weight,
            ],
            out_specs=[whole, whole, whole],
        ),
        out_shape=[wide, wide, jax.ShapeDtypeStruct((rows, hidden_units), BF)],
        name="forward_far",
    )(order, far, gate_near, up_near, gate_w, up_w)


def forward(order, near, far, gate_w, up_w):
    rows, half = near.shape
    hidden_units = gate_w.shape[1]
    step = half // 2

    def kernel(order_ref, near_ref, far_ref, gate_w_ref, up_w_ref, gate_ref, up_ref, hidden_ref):
        j = pl.program_id(0)

        @pl.when(j == 0)
        def _():
            gate_ref[...] = dot(near_ref[...], gate_w_ref[...])
            up_ref[...] = dot(near_ref[...], up_w_ref[...])

        @pl.when(j == 1)
        def _():
            gate_ref[...] += dot(near_ref[...], gate_w_ref[...])
            up_ref[...] += dot(near_ref[...], up_w_ref[...])

        @pl.when(j == 2)
        def _():
            gate_ref[...] += dot(far_ref[...], gate_w_ref[...])
            up_ref[...] += dot(far_ref[...], up_w_ref[...])

        @pl.when(j == 3)
        def _():
            gate = gate_ref[...] + dot(far_ref[...], gate_w_ref[...])
            up = up_ref[...] + dot(far_ref[...], up_w_ref[...])
            gate_ref[...] = gate
            up_ref[...] = up
            hidden_ref[...] = act_hidden(gate, up)

    whole = pl.BlockSpec((rows, hidden_units), lambda j, order_ref: (0, 0))
    weight = pl.BlockSpec((step, hidden_units), lambda j, order_ref: (order_ref[j], 0))
    return pl.pallas_call(
        kernel,
        grid_spec=pltpu.PrefetchScalarGridSpec(
            num_scalar_prefetch=1,
            grid=(4,),
            in_specs=[
                pl.BlockSpec((rows, step), lambda j, order_ref: (0, jnp.minimum(j, 1))),
                pl.BlockSpec((rows, step), lambda j, order_ref: (0, jnp.maximum(j - 2, 0))),
                weight,
                weight,
            ],
            out_specs=[whole, whole, whole],
        ),
        out_shape=[
            jax.ShapeDtypeStruct((rows, hidden_units), F32),
            jax.ShapeDtypeStruct((rows, hidden_units), F32),
            jax.ShapeDtypeStruct((rows, hidden_units), BF),
        ],
        name="forward",
    )(order, near, far, gate_w, up_w)


def partner_part(grad_rows, down_a, down_ab):
    rows, half = grad_rows.shape
    hidden_units = down_a.shape[0]

    def kernel(c_hbm, first_hbm, second_hbm, out_ref, c_ref, first_ref, second_ref, sem):
        c_copy = pltpu.make_async_copy(c_hbm, c_ref, sem.at[0])
        first = pltpu.make_async_copy(first_hbm, first_ref, sem.at[1])
        second = pltpu.make_async_copy(second_hbm, second_ref, sem.at[2])
        c_copy.start()
        first.start()
        second.start()
        c_copy.wait()
        first.wait()
        out_ref[:, :hidden_units] = dot(c_ref[...], first_ref[...], 1, 1).astype(BF)
        second.wait()
        out_ref[:, hidden_units:] = dot(c_ref[...], second_ref[...], 1, 1).astype(BF)

    weight = pltpu.VMEM((hidden_units, half), BF)
    return pl.pallas_call(
        kernel,
        in_specs=[pl.BlockSpec(memory_space=pl.ANY)] * 3,
        out_shape=jax.ShapeDtypeStruct((rows, 2 * hidden_units), BF),
        scratch_shapes=[
            pltpu.VMEM((rows, half), BF),
            weight,
            weight,
            pltpu.SemaphoreType.DMA((3,)),
        ],
        name="partner_part",
    )(grad_rows, down_a, down_ab)


def mix_last(base, hidden_far, down_far, hidden_near, down_near):
    rows, half = base.shape
    step = half // 2

    def kernel(base_hbm, hf_hbm, df_hbm, hn_hbm, dn_hbm, out_ref, *refs):
        scratch, sem = refs[:5], refs[5]
        sources = (hf_hbm, df_hbm, hn_hbm, dn_hbm, base_hbm)
        copies = [
            pltpu.make_async_copy(source, target, sem.at[k])
            for k, (source, target) in enumerate(zip(sources, scratch))
        ]
        for copy in copies:
            copy.start()
        hf_ref, df_ref, hn_ref, dn_ref, base_ref = scratch
        for copy in copies:
            copy.wait()
        for n in range(2):
            block = slice(n * step, (n + 1) * step)
            value = dot(hf_ref[...], df_ref[:, block]) + dot(hn_ref[...], dn_ref[:, block])
            out_ref[:, block] = (base_ref[:, block] + value).astype(BF)

    operands = (hidden_far, down_far, hidden_near, down_near)
    return pl.pallas_call(
        kernel,
        in_specs=[pl.BlockSpec(memory_space=pl.ANY)] * 5,
        out_shape=jax.ShapeDtypeStruct((rows, half), BF),
        scratch_shapes=[
            *[pltpu.VMEM(x.shape, BF) for x in operands],
            pltpu.VMEM((rows, half), F32),
            pltpu.SemaphoreType.DMA((5,)),
        ],
        name="mix_last",
    )(base, *operands)


def gradients(order, grad_rows, received, first, second):
    rows, half = grad_rows.shape
    hidden_units = first[1].shape[1]
    step = half // 2

    def kernel(order_ref, c_hbm, in_hbm, *refs):
        sources, outs = (refs[:5], refs[5:10]), refs[10:15]
        far_ref = outs[4]
        c_ref, in_ref, scratch, sem = refs[15], refs[16], (refs[17:22], refs[22:27]), refs[27]
        copies = []

        def start(source, target):
            copy = pltpu.make_async_copy(source, target, sem.at[len(copies)])
            copy.start()
            copies.append(copy)
            return copy

        c_copy = start(c_hbm, c_ref)
        small = [[start(sources[0][k], scratch[0][k]) for k in range(3)]]
        in_copy = start(in_hbm, in_ref)
        small.append([start(sources[1][k], scratch[1][k]) for k in range(3)])
        large = [
            [
                start(
                    sources[s][3 + k].at[pl.ds(order_ref[2 + n] * step, step), :],
                    scratch[s][3 + k].at[pl.ds(n * step, step), :],
                )
                for s in range(2)
                for k in range(2)
            ]
            for n in range(2)
        ]
        c_copy.wait()
        for s in range(2):
            down_ref, gate_ref, up_ref = scratch[s][:3]
            gg_ref, ug_ref = outs[2 * s], outs[2 * s + 1]
            small[s][0].wait()
            hidden_grad = dot(c_ref[...], down_ref[...], 1, 1)
            for copy in small[s][1:]:
                copy.wait()
            if s == 0:
                in_copy.wait()
            part = in_ref[:, s * hidden_units : (s + 1) * hidden_units]
            hidden_grad = hidden_grad + part.astype(F32)
            gate = gate_ref[...]
            sig = jax.nn.sigmoid(gate)
            up_part = up_ref[...] * sig * (1.0 + gate * (1.0 - sig))
            gg_ref[...] = (hidden_grad * up_part).astype(BF)
            ug_ref[...] = (hidden_grad * (gate * sig)).astype(BF)
        for n in range(2):
            for copy in large[n]:
                copy.wait()
            block = pl.ds(n * step, step)
            value = dot(outs[0][...], scratch[0][3][block, :], 1, 1)
            value += dot(outs[1][...], scratch[0][4][block, :], 1, 1)
            value += dot(outs[2][...], scratch[1][3][block, :], 1, 1)
            value += dot(outs[3][...], scratch[1][4][block, :], 1, 1)
            far_ref[:, n * step : (n + 1) * step] = value.astype(BF)

    wide = pltpu.VMEM((rows, hidden_units), F32)
    weight = pltpu.VMEM((half, hidden_units), BF)
    one_slice = [
        pltpu.VMEM((hidden_units, half), BF),
        wide,
        wide,
        weight,
        weight,
    ]
    anywhere = pl.BlockSpec(memory_space=pl.ANY)
    grad = jax.ShapeDtypeStruct((rows, hidden_units), BF)
    return pl.pallas_call(
        kernel,
        in_specs=[pl.BlockSpec(memory_space=pltpu.SMEM)] + [anywhere] * 12,
        out_shape=[grad, grad, grad, grad, jax.ShapeDtypeStruct((rows, half), BF)],
        scratch_shapes=[
            pltpu.VMEM((rows, half), BF),
            pltpu.VMEM((rows, 2 * hidden_units), BF),
            *one_slice,
            *one_slice,
            pltpu.SemaphoreType.DMA((16,)),
        ],
        name="gradients",
    )(order, grad_rows, received, *first, *second)


def layer(tokens, expert_ids, route_weights, w_gate, w_up, w_down, cotangent):
    num_experts = lax.axis_size("expert")
    tok_rows, top = expert_ids.shape
    capacity = tok_rows * top * 4 // (num_experts * 3)
    slots = capacity // 2
    y = lax.axis_index("replica")
    odd = lax.axis_index("expert") & 1
    outer = y >> 1
    inner = ((y + 1) >> 1) & 1
    near_0 = jnp.where(odd == 0, 2 * outer, inner)
    near_1 = jnp.where(odd == 0, 2 * outer + 1, 3 - inner)
    far_0 = jnp.where(odd == 0, 2 - 2 * outer, 1 - inner)
    far_1 = jnp.where(odd == 0, 3 - 2 * outer, 2 + inner)
    order = jnp.stack([near_0, near_1, far_0, far_1])
    gate_w, up_w, down_w = w_gate[0], w_up[0], w_down[0]

    gate_b = swap_b(gate_w)
    up_b = swap_b(up_w)
    down_own = columns(down_w, near_0, near_1)
    down_far = columns(down_w, far_0, far_1)
    down_a = swap_a(down_far)
    down_ab = swap_b(down_a)
    down_b = swap_b(down_own)

    experts = jnp.arange(num_experts, dtype=jnp.int32)
    hit = expert_ids.T[None, :, :] == experts[:, None, None]
    chosen = jnp.sum(hit.astype(F32), axis=1)
    weight = jnp.sum(jnp.where(hit, route_weights.T[None, :, :], 0.0), axis=1)
    before = jnp.arange(tok_rows)[:, None] < jnp.arange(tok_rows)[None, :]
    rank = dot(chosen.astype(BF), before.astype(BF))
    is_odd = (experts & 1)[:, None] == 1
    first_slot = slots * jnp.where(is_odd, outer, inner)
    place = jnp.where(chosen > 0, rank.astype(jnp.int32) - first_slot, -1)
    pick = place[:, None, :] == jnp.arange(slots, dtype=jnp.int32)[None, :, None]
    pick_w = jnp.where(pick, weight[:, None, :], 0.0)
    slot_weight = jnp.sum(pick_w, axis=2).reshape(-1, 1)
    is_odd = is_odd[:, :, None]

    def by_parity(value):
        parts = [jnp.where(is_odd, 0, value), jnp.where(is_odd, value, 0)]
        return jnp.concatenate(parts, axis=2).reshape(-1, 2 * tok_rows)

    pick = by_parity(pick.astype(BF))
    pick_hi = pick_w.astype(BF)
    pick_lo = by_parity((pick_w - pick_hi.astype(F32)).astype(BF))
    pick_hi = by_parity(pick_hi)

    def both(value):
        even = columns(value, 2 * outer, 2 * outer + 1)
        return jnp.concatenate([even, columns(value, inner, 3 - inner)], axis=0)

    packed = dot(pick, both(tokens)).astype(BF)
    rows_near = exchange(packed, num_experts)
    rows_far = swap_a(rows_near)
    packed_grad = (dot(pick, both(cotangent)) * slot_weight).astype(BF)
    grad_rows = exchange(packed_grad, num_experts)

    gate_n, up_n = forward_near(order, rows_near, gate_w, up_w)
    gate_1, up_1, hidden_1 = forward_far(order, rows_far, gate_n, up_n, gate_w, up_w)
    gate_2, up_2, hidden_2 = forward(order, rows_near, rows_far, gate_b, up_b)
    hidden_3 = swap_a(hidden_1)
    hidden_4 = swap_a(hidden_2)
    hgrad = partner_part(grad_rows, down_a, down_ab)
    hgrad = swap_a(hgrad)

    mixed_rows = dot(hidden_1, down_own) + dot(hidden_3, down_a)
    mixed_rows = lax.optimization_barrier(mixed_rows)
    mixed_rows = mix_last(mixed_rows, hidden_4, down_ab, hidden_2, down_b)
    mixed_back = exchange(mixed_rows, num_experts)

    gg_1, ug_1, gg_2, ug_2, far = gradients(
        order,
        grad_rows,
        hgrad,
        (down_own, gate_1, up_1, gate_w, up_w),
        (down_b, gate_2, up_2, gate_b, up_b),
    )
    far = swap_a(far)
    gate_1n = rows_of(gate_w, near_0, near_1)
    up_1n = rows_of(up_w, near_0, near_1)
    gate_2n = rows_of(gate_b, near_0, near_1)
    up_2n = rows_of(up_b, near_0, near_1)
    near = dot(gg_1, gate_1n, 1, 1) + dot(ug_1, up_1n, 1, 1)
    near = near + dot(gg_2, gate_2n, 1, 1) + dot(ug_2, up_2n, 1, 1)
    near = lax.optimization_barrier(near)
    near = (near + far.astype(F32)).astype(BF)
    grad_back = exchange(near, num_experts)

    def finish(partial):
        def share(value, at, pairs):
            low, high = jnp.split(value, 2, axis=1)
            keep = jnp.where(at == 0, low, high)
            give = jnp.where(at == 0, high, low).astype(BF)
            return keep + lax.ppermute(give, "replica", list(enumerate(pairs))).astype(F32)

        even, odd_part = jnp.split(partial, 2, axis=0)
        total = share(even, y & 1, PAIRS_0) + share(odd_part, outer, PAIRS_1)
        return total.astype(BF)

    mixed = finish(dot(pick_hi, mixed_back, 0, 0) + dot(pick_lo, mixed_back, 0, 0))
    tokens_grad = finish(dot(pick, grad_back, 0, 0))
    return (mixed, tokens_grad)


def solution(mesh):
    in_specs = (
        P("expert", None),
        P("expert", None),
        P("expert", None),
        P("expert", None, "replica"),
        P("expert", None, "replica"),
        P("expert", "replica", None),
        P("expert", None),
    )
    out_specs = (P("expert", "replica"), P("expert", "replica"))
    return jax.shard_map(layer, mesh=mesh, in_specs=in_specs, out_specs=out_specs, check_vma=False)
```

```python
import jax
import jax.numpy as jnp
from jax import lax
from jax.experimental import pallas as pl
from jax.experimental.pallas import tpu as pltpu
from jax.sharding import PartitionSpec as P


BF = jnp.bfloat16
F32 = jnp.float32
PAIRS_0 = (1, 0, 3, 2)
PAIRS_1 = (3, 2, 1, 0)


def swap(value, even, odd):
    pairs = []
    for expert in range(lax.axis_size("expert")):
        partner = odd if expert % 2 else even
        pairs += [(expert * 4 + y, expert * 4 + partner[y]) for y in range(4)]
    return lax.ppermute(value, ("expert", "replica"), pairs)


def swap_b(value):
    return swap(value, PAIRS_0, PAIRS_1)


def swap_a(value):
    return swap(value, PAIRS_1, PAIRS_0)


def dot(lhs, rhs, ldim=1, rdim=0):
    return lax.dot_general(lhs, rhs, (((ldim,), (rdim,)), ((), ())), preferred_element_type=F32)


def choose(value, index):
    quarters = jnp.split(value, 4, axis=1)
    low = jnp.where(index == 0, quarters[0], quarters[1])
    high = jnp.where(index == 2, quarters[2], quarters[3])
    return jnp.where(index < 2, low, high)


def columns(value, first, second):
    return jnp.concatenate([choose(value, first), choose(value, second)], axis=1)


def rows_of(value, first, second):
    size = value.shape[0] // 4
    return jnp.concatenate(
        [
            lax.dynamic_slice_in_dim(value, first * size, size, 0),
            lax.dynamic_slice_in_dim(value, second * size, size, 0),
        ],
        axis=0,
    )


def exchange(rows, num_experts):
    width = rows.shape[1]
    moved = lax.all_to_all(
        rows.reshape(num_experts, -1, width), "expert", split_axis=0, concat_axis=0, tiled=True
    )
    return moved.reshape(-1, width)


def act_hidden(gate, up):
    return (gate * jax.nn.sigmoid(gate) * up).astype(BF)


def forward_near(order, near, gate_w, up_w):
    rows, half = near.shape
    hidden_units = gate_w.shape[1]
    step = half // 2

    def kernel(order_ref, near_ref, gate_w_ref, up_w_ref, gate_ref, up_ref):
        gate = dot(near_ref[...], gate_w_ref[...])
        up = dot(near_ref[...], up_w_ref[...])

        @pl.when(pl.program_id(0) == 0)
        def _():
            gate_ref[...] = gate
            up_ref[...] = up

        @pl.when(pl.program_id(0) == 1)
        def _():
            gate_ref[...] += gate
            up_ref[...] += up

    whole = pl.BlockSpec((rows, hidden_units), lambda j, order_ref: (0, 0))
    weight = pl.BlockSpec((step, hidden_units), lambda j, order_ref: (order_ref[j], 0))
    return pl.pallas_call(
        kernel,
        grid_spec=pltpu.PrefetchScalarGridSpec(
            num_scalar_prefetch=1,
            grid=(2,),
            in_specs=[pl.BlockSpec((rows, step), lambda j, order_ref: (0, j)), weight, weight],
            out_specs=[whole, whole],
        ),
        out_shape=[jax.ShapeDtypeStruct((rows, hidden_units), F32)] * 2,
        name="forward_near",
    )(order, near, gate_w, up_w)


def forward_far(order, far, gate_near, up_near, gate_w, up_w):
    rows, half = far.shape
    hidden_units = gate_w.shape[1]
    step = half // 2

    def kernel(order_ref, far_ref, gn_ref, un_ref, gate_w_ref, up_w_ref, gate_ref, up_ref, hidden_ref):
        @pl.when(pl.program_id(0) == 0)
        def _():
            gate_ref[...] = gn_ref[...] + dot(far_ref[...], gate_w_ref[...])
            up_ref[...] = un_ref[...] + dot(far_ref[...], up_w_ref[...])

        @pl.when(pl.program_id(0) == 1)
        def _():
            gate = gate_ref[...] + dot(far_ref[...], gate_w_ref[...])
            up = up_ref[...] + dot(far_ref[...], up_w_ref[...])
            gate_ref[...] = gate
            up_ref[...] = up
            hidden_ref[...] = act_hidden(gate, up)

    whole = pl.BlockSpec((rows, hidden_units), lambda j, order_ref: (0, 0))
    weight = pl.BlockSpec((step, hidden_units), lambda j, order_ref: (order_ref[2 + j], 0))
    wide = jax.ShapeDtypeStruct((rows, hidden_units), F32)
    return pl.pallas_call(
        kernel,
        grid_spec=pltpu.PrefetchScalarGridSpec(
            num_scalar_prefetch=1,
            grid=(2,),
            in_specs=[
                pl.BlockSpec((rows, step), lambda j, order_ref: (0, j)),
                whole,
                whole,
                weight,
                weight,
            ],
            out_specs=[whole, whole, whole],
        ),
        out_shape=[wide, wide, jax.ShapeDtypeStruct((rows, hidden_units), BF)],
        name="forward_far",
    )(order, far, gate_near, up_near, gate_w, up_w)


def forward(order, near, far, gate_w, up_w):
    rows, half = near.shape
    hidden_units = gate_w.shape[1]
    step = half // 2

    def kernel(order_ref, near_ref, far_ref, gate_w_ref, up_w_ref, gate_ref, up_ref, hidden_ref):
        j = pl.program_id(0)

        @pl.when(j == 0)
        def _():
            gate_ref[...] = dot(near_ref[...], gate_w_ref[...])
            up_ref[...] = dot(near_ref[...], up_w_ref[...])

        @pl.when(j == 1)
        def _():
            gate_ref[...] += dot(near_ref[...], gate_w_ref[...])
            up_ref[...] += dot(near_ref[...], up_w_ref[...])

        @pl.when(j == 2)
        def _():
            gate_ref[...] += dot(far_ref[...], gate_w_ref[...])
            up_ref[...] += dot(far_ref[...], up_w_ref[...])

        @pl.when(j == 3)
        def _():
            gate = gate_ref[...] + dot(far_ref[...], gate_w_ref[...])
            up = up_ref[...] + dot(far_ref[...], up_w_ref[...])
            gate_ref[...] = gate
            up_ref[...] = up
            hidden_ref[...] = act_hidden(gate, up)

    whole = pl.BlockSpec((rows, hidden_units), lambda j, order_ref: (0, 0))
    weight = pl.BlockSpec((step, hidden_units), lambda j, order_ref: (order_ref[j], 0))
    return pl.pallas_call(
        kernel,
        grid_spec=pltpu.PrefetchScalarGridSpec(
            num_scalar_prefetch=1,
            grid=(4,),
            in_specs=[
                pl.BlockSpec((rows, step), lambda j, order_ref: (0, jnp.minimum(j, 1))),
                pl.BlockSpec((rows, step), lambda j, order_ref: (0, jnp.maximum(j - 2, 0))),
                weight,
                weight,
            ],
            out_specs=[whole, whole, whole],
        ),
        out_shape=[
            jax.ShapeDtypeStruct((rows, hidden_units), F32),
            jax.ShapeDtypeStruct((rows, hidden_units), F32),
            jax.ShapeDtypeStruct((rows, hidden_units), BF),
        ],
        name="forward",
    )(order, near, far, gate_w, up_w)


def partner_part(grad_rows, down_a, down_ab):
    rows, half = grad_rows.shape
    hidden_units = down_a.shape[0]

    def kernel(c_hbm, first_hbm, second_hbm, out_ref, c_ref, first_ref, second_ref, sem):
        c_copy = pltpu.make_async_copy(c_hbm, c_ref, sem.at[0])
        first = pltpu.make_async_copy(first_hbm, first_ref, sem.at[1])
        second = pltpu.make_async_copy(second_hbm, second_ref, sem.at[2])
        c_copy.start()
        first.start()
        second.start()
        c_copy.wait()
        first.wait()
        out_ref[:, :hidden_units] = dot(c_ref[...], first_ref[...], 1, 1).astype(BF)
        second.wait()
        out_ref[:, hidden_units:] = dot(c_ref[...], second_ref[...], 1, 1).astype(BF)

    weight = pltpu.VMEM((hidden_units, half), BF)
    return pl.pallas_call(
        kernel,
        in_specs=[pl.BlockSpec(memory_space=pl.ANY)] * 3,
        out_shape=jax.ShapeDtypeStruct((rows, 2 * hidden_units), BF),
        scratch_shapes=[
            pltpu.VMEM((rows, half), BF),
            weight,
            weight,
            pltpu.SemaphoreType.DMA((3,)),
        ],
        name="partner_part",
    )(grad_rows, down_a, down_ab)


def gradients(order, grad_rows, received, first, second):
    rows, half = grad_rows.shape
    hidden_units = first[1].shape[1]
    step = half // 2

    def kernel(order_ref, c_hbm, in_hbm, *refs):
        sources, outs = (refs[:5], refs[5:10]), refs[10:15]
        far_ref = outs[4]
        c_ref, in_ref, scratch, sem = refs[15], refs[16], (refs[17:22], refs[22:27]), refs[27]
        copies = []

        def start(source, target):
            copy = pltpu.make_async_copy(source, target, sem.at[len(copies)])
            copy.start()
            copies.append(copy)
            return copy

        c_copy = start(c_hbm, c_ref)
        small = [[start(sources[0][k], scratch[0][k]) for k in range(3)]]
        in_copy = start(in_hbm, in_ref)
        small.append([start(sources[1][k], scratch[1][k]) for k in range(3)])
        large = [
            [
                start(
                    sources[s][3 + k].at[pl.ds(order_ref[2 + n] * step, step), :],
                    scratch[s][3 + k].at[pl.ds(n * step, step), :],
                )
                for s in range(2)
                for k in range(2)
            ]
            for n in range(2)
        ]
        c_copy.wait()
        for s in range(2):
            down_ref, gate_ref, up_ref = scratch[s][:3]
            gg_ref, ug_ref = outs[2 * s], outs[2 * s + 1]
            small[s][0].wait()
            hidden_grad = dot(c_ref[...], down_ref[...], 1, 1)
            for copy in small[s][1:]:
                copy.wait()
            if s == 0:
                in_copy.wait()
            part = in_ref[:, s * hidden_units : (s + 1) * hidden_units]
            hidden_grad = hidden_grad + part.astype(F32)
            gate = gate_ref[...]
            sig = jax.nn.sigmoid(gate)
            up_part = up_ref[...] * sig * (1.0 + gate * (1.0 - sig))
            gg_ref[...] = (hidden_grad * up_part).astype(BF)
            ug_ref[...] = (hidden_grad * (gate * sig)).astype(BF)
        for n in range(2):
            for copy in large[n]:
                copy.wait()
            block = pl.ds(n * step, step)
            value = dot(outs[0][...], scratch[0][3][block, :], 1, 1)
            value += dot(outs[1][...], scratch[0][4][block, :], 1, 1)
            value += dot(outs[2][...], scratch[1][3][block, :], 1, 1)
            value += dot(outs[3][...], scratch[1][4][block, :], 1, 1)
            far_ref[:, n * step : (n + 1) * step] = value.astype(BF)

    wide = pltpu.VMEM((rows, hidden_units), F32)
    weight = pltpu.VMEM((half, hidden_units), BF)
    one_slice = [
        pltpu.VMEM((hidden_units, half), BF),
        wide,
        wide,
        weight,
        weight,
    ]
    anywhere = pl.BlockSpec(memory_space=pl.ANY)
    grad = jax.ShapeDtypeStruct((rows, hidden_units), BF)
    return pl.pallas_call(
        kernel,
        in_specs=[pl.BlockSpec(memory_space=pltpu.SMEM)] + [anywhere] * 12,
        out_shape=[grad, grad, grad, grad, jax.ShapeDtypeStruct((rows, half), BF)],
        scratch_shapes=[
            pltpu.VMEM((rows, half), BF),
            pltpu.VMEM((rows, 2 * hidden_units), BF),
            *one_slice,
            *one_slice,
            pltpu.SemaphoreType.DMA((16,)),
        ],
        name="gradients",
    )(order, grad_rows, received, *first, *second)


def layer(tokens, expert_ids, route_weights, w_gate, w_up, w_down, cotangent):
    num_experts = lax.axis_size("expert")
    tok_rows, top = expert_ids.shape
    capacity = tok_rows * top * 4 // (num_experts * 3)
    slots = capacity // 2
    y = lax.axis_index("replica")
    odd = lax.axis_index("expert") & 1
    outer = y >> 1
    inner = ((y + 1) >> 1) & 1
    near_0 = jnp.where(odd == 0, 2 * outer, inner)
    near_1 = jnp.where(odd == 0, 2 * outer + 1, 3 - inner)
    far_0 = jnp.where(odd == 0, 2 - 2 * outer, 1 - inner)
    far_1 = jnp.where(odd == 0, 3 - 2 * outer, 2 + inner)
    order = jnp.stack([near_0, near_1, far_0, far_1])
    gate_w, up_w, down_w = w_gate[0], w_up[0], w_down[0]

    gate_b = swap_b(gate_w)
    up_b = swap_b(up_w)
    down_own = columns(down_w, near_0, near_1)
    down_far = columns(down_w, far_0, far_1)
    down_a = swap_a(down_far)
    down_ab = swap_b(down_a)
    down_b = swap_b(down_own)

    experts = jnp.arange(num_experts, dtype=jnp.int32)
    hit = expert_ids.T[None, :, :] == experts[:, None, None]
    chosen = jnp.sum(hit.astype(F32), axis=1)
    weight = jnp.sum(jnp.where(hit, route_weights.T[None, :, :], 0.0), axis=1)
    before = jnp.arange(tok_rows)[:, None] < jnp.arange(tok_rows)[None, :]
    rank = dot(chosen.astype(BF), before.astype(BF))
    is_odd = (experts & 1)[:, None] == 1
    first_slot = slots * jnp.where(is_odd, outer, inner)
    place = jnp.where(chosen > 0, rank.astype(jnp.int32) - first_slot, -1)
    pick = place[:, None, :] == jnp.arange(slots, dtype=jnp.int32)[None, :, None]
    pick_w = jnp.where(pick, weight[:, None, :], 0.0)
    slot_weight = jnp.sum(pick_w, axis=2).reshape(-1, 1)
    is_odd = is_odd[:, :, None]

    def by_parity(value):
        parts = [jnp.where(is_odd, 0, value), jnp.where(is_odd, value, 0)]
        return jnp.concatenate(parts, axis=2).reshape(-1, 2 * tok_rows)

    pick = by_parity(pick.astype(BF))
    pick_hi = pick_w.astype(BF)
    pick_lo = by_parity((pick_w - pick_hi.astype(F32)).astype(BF))
    pick_hi = by_parity(pick_hi)

    def both(value):
        even = columns(value, 2 * outer, 2 * outer + 1)
        return jnp.concatenate([even, columns(value, inner, 3 - inner)], axis=0)

    packed = dot(pick, both(tokens)).astype(BF)
    rows_near = exchange(packed, num_experts)
    rows_far = swap_a(rows_near)
    packed_grad = (dot(pick, both(cotangent)) * slot_weight).astype(BF)
    grad_rows = exchange(packed_grad, num_experts)

    gate_n, up_n = forward_near(order, rows_near, gate_w, up_w)
    gate_1, up_1, hidden_1 = forward_far(order, rows_far, gate_n, up_n, gate_w, up_w)
    gate_2, up_2, hidden_2 = forward(order, rows_near, rows_far, gate_b, up_b)
    hidden_3 = swap_a(hidden_1)
    hidden_4 = swap_a(hidden_2)
    hgrad = partner_part(grad_rows, down_a, down_ab)
    hgrad = swap_a(hgrad)

    mixed_rows = dot(hidden_1, down_own) + dot(hidden_3, down_a)
    mixed_rows = lax.optimization_barrier(mixed_rows)
    mixed_rows = lax.optimization_barrier(mixed_rows + dot(hidden_4, down_ab))
    mixed_rows = (mixed_rows + dot(hidden_2, down_b)).astype(BF)
    mixed_back = exchange(mixed_rows, num_experts)

    gg_1, ug_1, gg_2, ug_2, far = gradients(
        order,
        grad_rows,
        hgrad,
        (down_own, gate_1, up_1, gate_w, up_w),
        (down_b, gate_2, up_2, gate_b, up_b),
    )
    far = swap_a(far)
    gate_1n = rows_of(gate_w, near_0, near_1)
    up_1n = rows_of(up_w, near_0, near_1)
    gate_2n = rows_of(gate_b, near_0, near_1)
    up_2n = rows_of(up_b, near_0, near_1)
    near = dot(gg_1, gate_1n, 1, 1) + dot(ug_1, up_1n, 1, 1)
    near = near + dot(gg_2, gate_2n, 1, 1) + dot(ug_2, up_2n, 1, 1)
    near = lax.optimization_barrier(near)
    near = (near + far.astype(F32)).astype(BF)
    grad_back = exchange(near, num_experts)

    def finish(partial):
        def share(value, at, pairs):
            low, high = jnp.split(value, 2, axis=1)
            keep = jnp.where(at == 0, low, high)
            give = jnp.where(at == 0, high, low).astype(BF)
            return keep + lax.ppermute(give, "replica", list(enumerate(pairs))).astype(F32)

        even, odd_part = jnp.split(partial, 2, axis=0)
        total = share(even, y & 1, PAIRS_0) + share(odd_part, outer, PAIRS_1)
        return total.astype(BF)

    mixed = finish(dot(pick_hi, mixed_back, 0, 0) + dot(pick_lo, mixed_back, 0, 0))
    tokens_grad = finish(dot(pick, grad_back, 0, 0))
    return (mixed, tokens_grad)


def solution(mesh):
    in_specs = (
        P("expert", None),
        P("expert", None),
        P("expert", None),
        P("expert", None, "replica"),
        P("expert", None, "replica"),
        P("expert", "replica", None),
        P("expert", None),
    )
    out_specs = (P("expert", "replica"), P("expert", "replica"))
    return jax.shard_map(layer, mesh=mesh, in_specs=in_specs, out_specs=out_specs, check_vma=False)
```
